1024 devices in a mesh: gz: 64 (over y_lo, z), gx: 4 (over y_hi, core), gy: 4 (over x).
Axes of the slice: x: 4, y: 8 (y_hi: 2, y_lo: 4; y = y_hi * 4 + y_lo), z: 16, core: 2. Of those that a mesh axis runs over, the one named last changes fastest.
Arguments:
- fields_in: float32 [6, 256, 256, 512], P(None, 'gz', 'gx', 'gy'), may hold values from -6 to 6
- material: int32 [256, 256, 512], P('gz', 'gx', 'gy'), may hold values from 0 to 3, as said below
- material_eps: float32 [4], replicated, may hold values from 1 to 12
- source_plane: int32 [1], replicated, may hold values from 0 to 255
- source_wave: float32 [4], replicated, may hold values from -8 to 8
- source_profile: float32 [256, 512], P('gx', 'gy'), may hold values from -6 to 6
- forward_fields: bfloat16 [4, 3, 256, 256, 512], P(None, None, 'gz', 'gx', 'gy'), may hold values from -6 to 6
Outputs:
- fields_out: float32 [6, 256, 256, 512], P(None, 'gz', 'gx', 'gy')
- eps_grad: float32 [256, 256, 512], P('gz', 'gx', 'gy')
The draws below stay inside these ranges and needn't reach their ends.
Inputs may be any that keep to these rules, and one draw needn't show every extreme that they name: `material`: planes z below 96 hold index 1; planes from 160 up hold index 0; the planes between hold 0 or an index of 2 to 3 in each cell.
All inputs are finite; a program needn't handle non-finite values.
Results may differ from the reference program's by a relative error of at most 0.0003.
Values sent between devices are 32-bit elements; how exact they have to be, the bound alone decides.
A program may use at most 64 MiB of HBM per device.

```python
import jax
import jax.numpy as jnp

STEPS = 4
NMAT = 4
NX = 256
NY = 512
NZ = 256


def draw_material(key, part):
    zpos = jnp.arange(NZ)[:, None, None]
    lower = NZ // 2 - NZ // 8
    upper = NZ // 2 + NZ // 8
    picked = jax.random.randint(key, (NZ, NX, NY), 0, NMAT - 1)
    pillar = jnp.where(picked == 0, 0, picked + 1)
    layered = jnp.where(zpos < lower, 1, jnp.where(zpos < upper, pillar, 0))
    layered = layered.at[lower, 0, 0].set(NMAT - 1)
    return layered.astype(jnp.int32)


def levels(key, dims, pieces, least, top_value):
    def one(axis_at, parts):
        steps = jax.random.uniform(jax.random.fold_in(jax.random.fold_in(key, 6), axis_at), (parts,), jnp.float32, least / len(pieces), top_value / len(pieces))
        return jnp.repeat(jnp.exp(steps), dims[axis_at] // parts).reshape((-1,) + (1,) * (len(dims) - axis_at - 1))

    loudness = one(*pieces[0])
    for cut in pieces[1:]:
        loudness = loudness * one(*cut)
    return loudness


def normal_values(rng, shape, spread, limit, pieces=(), dtype=jnp.bfloat16):
    values = jax.random.normal(rng, shape, jnp.float32) * spread
    if len(pieces) > 0:
        values = levels(rng, shape, pieces, -0.22, 0.18) * values
    return jnp.clip(values, min=-limit, max=limit).astype(dtype)


def setup_inputs(seed: int = 0) -> dict:
    keys = jax.random.split(jax.random.key(seed), 8)
    return {
        "fields_in": normal_values(keys[0], (6, NZ, NX, NY), 1.0, 6.0, ((1, 64), (2, 4), (3, 4)), jnp.float32),
        "material": draw_material(jax.random.fold_in(keys[7], 71), 0),
        "material_eps": jnp.clip(jax.random.uniform(keys[2], (NMAT,), jnp.float32, 1.0, 12.0), 1.0, 12.0),
        "source_plane": jax.random.randint(keys[3], (1,), 0, NZ).astype(jnp.int32),
        "source_wave": normal_values(keys[4], (STEPS,), 2.0, 8.0, (), jnp.float32),
        "source_profile": normal_values(keys[5], (NX, NY), 1.0, 6.0, ((0, 4), (1, 4)), jnp.float32),
        "forward_fields": normal_values(keys[6], (STEPS, 3, NZ, NX, NY), 1.0, 6.0, ((2, 64), (3, 4), (4, 4))),
    }


COURANT = 0.5


def z_after(field):
    return jnp.concatenate([field[1:], jnp.zeros_like(field[:1])], axis=0)


def z_before(field):
    return jnp.concatenate([jnp.zeros_like(field[:1]), field[:-1]], axis=0)


def reference(fields_in, material, material_eps, source_plane, source_wave, source_profile, forward_fields):
    permit = material_eps[material]
    coef = COURANT / permit
    depth = material.shape[0]
    zpos = jnp.arange(depth).astype(jnp.int32)
    source = jnp.where(zpos == source_plane[0], 1.0, 0.0).astype(jnp.float32)[:, None, None] * source_profile[None]
    elec_x, elec_y, elec_z = fields_in[0], fields_in[1], fields_in[2]
    magn_x, magn_y, magn_z = fields_in[3], fields_in[4], fields_in[5]
    grad = jnp.zeros(material.shape, jnp.float32)
    for instant in range(source_wave.shape[0]):
        curl_x = (jnp.roll(elec_z, -1, 2) - elec_z) - (z_after(elec_y) - elec_y)
        curl_y = (z_after(elec_x) - elec_x) - (jnp.roll(elec_z, -1, 1) - elec_z)
        curl_z = (jnp.roll(elec_y, -1, 1) - elec_y) - (jnp.roll(elec_x, -1, 2) - elec_x)
        magn_x = magn_x - COURANT * curl_x
        magn_y = magn_y - COURANT * curl_y
        magn_z = magn_z - COURANT * curl_z
        back_x = (magn_z - jnp.roll(magn_z, 1, 2)) - (magn_y - z_before(magn_y))
        back_y = (magn_x - z_before(magn_x)) - (magn_z - jnp.roll(magn_z, 1, 1))
        back_z = (magn_y - jnp.roll(magn_y, 1, 1)) - (magn_x - jnp.roll(magn_x, 1, 2))
        elec_x = elec_x + coef * back_x + coef * source_wave[instant] * source
        elec_y = elec_y + coef * back_y
        elec_z = elec_z + coef * back_z
        stored = forward_fields[instant].astype(jnp.float32)
        grad = grad + stored[0] * elec_x + stored[1] * elec_y + stored[2] * elec_z
    fields_out = jnp.stack([elec_x, elec_y, elec_z, magn_x, magn_y, magn_z])
    eps_grad = jnp.where(material >= 2, -grad, 0.0).astype(jnp.float32)
    return fields_out, eps_grad
```

```python
import functools

import jax
import jax.numpy as jnp
from jax import lax
from jax.experimental import pallas as pl
from jax.experimental.pallas import tpu as pltpu
from jax.sharding import PartitionSpec as P

COURANT = 0.5
MESH = pl.DeviceIdType.MESH
AXES = ("gz", "gx", "gy")


def around(axis, by):
    size = lax.axis_size(axis)
    return lax.rem(lax.axis_index(axis) + by + size, size)


def half_copies(field, row, packed, zghost, xghost, yghost, send, recv, slot, by):
    pieces = (
        (field.at[pl.ds(row, 2), 0 if by < 0 else field.shape[1] - 1], zghost.at[slot], "gz"),
        (
            field.at[
                pl.ds(row + 1, 2), :, pl.ds(0 if by < 0 else field.shape[2] - 8, 8)
            ],
            xghost.at[slot],
            "gx",
        ),
        (packed.at[slot], yghost.at[slot], "gy"),
    )
    return [
        pltpu.make_async_remote_copy(
            src_ref=src,
            dst_ref=dst,
            send_sem=send.at[slot, k],
            recv_sem=recv.at[slot, k],
            device_id={axis: around(axis, by)},
            device_id_type=MESH,
        )
        for k, (src, dst, axis) in enumerate(pieces)
    ]


def kernel(
    steps,
    eps_ref,
    plane_ref,
    wave_ref,
    fields_ref,
    material_ref,
    profile_ref,
    forward_ref,
    out_ref,
    grad_ref,
    coef_ref,
    packed,
    zghost,
    xghost,
    yghost,
    send,
    recv,
):
    _, depth, rows, lanes = fields_ref.shape
    gz, last = lax.axis_index("gz"), lax.axis_size("gz") - 1

    barrier = pltpu.get_barrier_semaphore()
    for axis in AXES:
        for by in (1, -1):
            pl.semaphore_signal(
                barrier, inc=1, device_id={axis: around(axis, by)}, device_id_type=MESH
            )

    for p in range(depth):
        kinds = material_ref[p]
        permit = jnp.full(kinds.shape, eps_ref[0], jnp.float32)
        for which in range(1, eps_ref.shape[0]):
            permit = jnp.where(kinds == which, eps_ref[which], permit)
        coef_ref[p] = COURANT / permit

    lane = lax.broadcasted_iota(jnp.int32, (rows, lanes), 1)
    row = lax.broadcasted_iota(jnp.int32, (rows, lanes), 0)

    def pack(ref, names, slot, shift):
        out = jnp.zeros((rows, lanes), jnp.float32)
        q = 0
        for c in names:
            for p in range(depth):
                v = ref[c, p]
                turn = (q + shift) % lanes
                out = jnp.where(lane == q, pltpu.roll(v, turn, 1) if turn else v, out)
                q += 1
        packed[slot] = out

    def start(copies, by):
        edge = 0 if by < 0 else last

        @pl.when(gz != edge)
        def _():
            copies[0].start()

        copies[1].start()
        copies[2].start()

    def finish(copies, by, slot):
        edge = last if by < 0 else 0

        @pl.when(gz != edge)
        def _():
            copies[0].wait_recv()

        @pl.when(gz == edge)
        def _():
            zghost[slot] = jnp.zeros(zghost.shape[1:], jnp.float32)

        copies[1].wait_recv()
        copies[2].wait_recv()

    def sent(copies, by):
        edge = 0 if by < 0 else last

        @pl.when(gz != edge)
        def _():
            copies[0].wait_send()

        copies[1].wait_send()
        copies[2].wait_send()

    pack(fields_ref, (0, 2), 0, 0)
    pl.semaphore_wait(barrier, 2 * len(AXES))
    pending = half_copies(fields_ref, 0, packed, zghost, xghost, yghost, send, recv, 0, -1)
    start(pending, -1)

    for t in range(steps):
        now = fields_ref if t == 0 else out_ref
        slot = 2 * t
        finish(pending, -1, slot)

        def after_x(c, p):
            v = now[c, p]
            border = jnp.broadcast_to(xghost[slot, c - 1, p, 0:1], v.shape)
            return jnp.where(row == rows - 1, border, pltpu.roll(v, rows - 1, 0)) - v

        def after_y(c, p):
            v = now[c, p]
            q = p if c == 0 else depth + p
            border = pltpu.roll(yghost[slot], lanes - 1 - q, 1)
            return jnp.where(lane == lanes - 1, border, pltpu.roll(v, lanes - 1, 1)) - v

        def after_z(c, p):
            following = now[c, p + 1] if p + 1 < depth else zghost[slot, c]
            return following - now[c, p]

        for p in range(depth - 1, -1, -1):
            out_ref[3, p] = now[3, p] - COURANT * (after_y(2, p) - after_z(1, p))
            out_ref[4, p] = now[4, p] - COURANT * (after_z(0, p) - after_x(2, p))
            out_ref[5, p] = now[5, p] - COURANT * (after_x(1, p) - after_y(0, p))
        pack(out_ref, (3, 5), slot + 1, 1)
        copies = half_copies(
            out_ref, 3, packed, zghost, xghost, yghost, send, recv, slot + 1, 1
        )
        start(copies, 1)
        sent(pending, -1)
        finish(copies, 1, slot + 1)

        def before_x(c, p):
            v = out_ref[c, p]
            border = jnp.broadcast_to(xghost[slot + 1, c - 4, p, 7:8], v.shape)
            return v - jnp.where(row == 0, border, pltpu.roll(v, 1, 0))

        def before_y(c, p):
            v = out_ref[c, p]
            q = p if c == 3 else depth + p
            border = yghost[slot + 1]
            border = pltpu.roll(border, lanes - q, 1) if q else border
            return v - jnp.where(lane == 0, border, pltpu.roll(v, 1, 1))

        def before_z(c, p):
            previous = out_ref[c, p - 1] if p > 0 else zghost[slot + 1, c - 3]
            return out_ref[c, p] - previous

        amplitude = wave_ref[t]
        for p in range(depth):
            coef = coef_ref[p]
            here = (gz * depth + p == plane_ref[0]).astype(jnp.float32)
            pushed = (amplitude * here) * profile_ref[...]
            out_ref[0, p] = now[0, p] + coef * (before_y(5, p) - before_z(4, p) + pushed)
            out_ref[1, p] = now[1, p] + coef * (before_z(3, p) - before_x(5, p))
            out_ref[2, p] = now[2, p] + coef * (before_x(4, p) - before_y(3, p))
        sent(copies, 1)
        if t + 1 < steps:
            pack(out_ref, (0, 2), slot + 2, 0)
            pending = half_copies(
                out_ref, 0, packed, zghost, xghost, yghost, send, recv, slot + 2, -1
            )
            start(pending, -1)
        for p in range(depth):
            total = jnp.zeros((rows, lanes), jnp.float32) if t == 0 else grad_ref[p]
            for c in range(3):
                total = total + forward_ref[t, c, p].astype(jnp.float32) * out_ref[c, p]
            if t + 1 == steps:
                total = jnp.where(material_ref[p] >= 2, -total, 0.0)
            grad_ref[p] = total


def on_device(
    fields_in, material, material_eps, source_plane, source_wave, source_profile, forward_fields
):
    depth, rows, lanes = material.shape
    steps = source_wave.shape[0]
    slots = 2 * steps
    whole = pl.BlockSpec(memory_space=pltpu.VMEM)
    scalars = pl.BlockSpec(memory_space=pltpu.SMEM)
    return pl.pallas_call(
        functools.partial(kernel, steps),
        out_shape=(
            jax.ShapeDtypeStruct(fields_in.shape, jnp.float32),
            jax.ShapeDtypeStruct(material.shape, jnp.float32),
        ),
        in_specs=[scalars] * 3 + [whole] * 4,
        out_specs=(whole, whole),
        scratch_shapes=[
            pltpu.VMEM((depth, rows, lanes), jnp.float32),
            pltpu.VMEM((slots, rows, lanes), jnp.float32),
            pltpu.VMEM((slots, 2, rows, lanes), jnp.float32),
            pltpu.VMEM((slots, 2, depth, 8, lanes), jnp.float32),
            pltpu.VMEM((slots, rows, lanes), jnp.float32),
            pltpu.SemaphoreType.DMA((slots, 3)),
            pltpu.SemaphoreType.DMA((slots, 3)),
        ],
        compiler_params=pltpu.CompilerParams(
            collective_id=0, has_side_effects=True, vmem_limit_bytes=32 << 20
        ),
    )(
        material_eps,
        source_plane,
        source_wave,
        fields_in,
        material,
        source_profile,
        forward_fields,
    )


def solution(mesh):
    placed = (
        P(None, "gz", "gx", "gy"),
        P("gz", "gx", "gy"),
        P(),
        P(),
        P(),
        P("gx", "gy"),
        P(None, None, "gz", "gx", "gy"),
    )
    return jax.shard_map(
        on_device,
        mesh=mesh,
        in_specs=placed,
        out_specs=(P(None, "gz", "gx", "gy"), P("gz", "gx", "gy")),
        check_vma=False,
    )
```

```python
import functools

import jax
import jax.numpy as jnp
from jax import lax
from jax.experimental import pallas as pl
from jax.experimental.pallas import tpu as pltpu
from jax.sharding import PartitionSpec as P

COURANT = 0.5
MESH = pl.DeviceIdType.MESH
AXES = ("gz", "gx", "gy")
STEPS = 4
LOW = 2
HALO = 4
SLOT = 2 * HALO
COPIES = 29


def around(axis, by):
    size = lax.axis_size(axis)
    return lax.rem(lax.axis_index(axis) + by + size, size)


class Copy:
    def __init__(self, k, src, dst, axis, by, send, recv):
        self.end = axis == "gz"
        last = lax.axis_size("gz") - 1
        self.sends = lax.axis_index("gz") != (last if by > 0 else 0)
        self.takes = lax.axis_index("gz") != (0 if by > 0 else last)
        self.copy = pltpu.make_async_remote_copy(
            src_ref=src,
            dst_ref=dst,
            send_sem=send.at[k],
            recv_sem=recv.at[k],
            device_id={axis: around(axis, by)},
            device_id_type=MESH,
        )

    def _on(self, flag, act):
        if self.end:
            pl.when(flag)(act)
        else:
            act()

    def start(self):
        self._on(self.sends, self.copy.start)

    def sent(self):
        self._on(self.sends, self.copy.wait_send)

    def arrived(self):
        self._on(self.takes, self.copy.wait_recv)


def each(planes, act):
    for p in planes:
        act(p)


def run(lo, hi, act):
    if hi - lo == 1:
        act(lo)
    else:
        lax.fori_loop(lo, hi, lambda p, _: (act(p), 0)[1], 0)


def kernel(
    eps_ref,
    plane_ref,
    wave_ref,
    fields,
    material,
    profile,
    forward,
    out_ref,
    grad_ref,
    fa,
    fb,
    ca,
    cb,
    mat,
    prof_a,
    prof_b,
    stored,
    packed,
    y_in,
    border,
    z_border,
    x_in,
    x_mat_in,
    x_prof_in,
    x_border_in,
    x_out,
    x_mat_out,
    said,
    heard,
    local,
    send,
    recv,
):
    _, depth, rows, lanes = fields.shape
    wide = rows + 2 * HALO
    own = pl.ds(0, rows)
    extra = pl.ds(rows, 2 * HALO)
    first, final = pl.ds(0, 8), pl.ds(rows - 8, 8)
    top = LOW + depth
    gz, last = lax.axis_index("gz"), lax.axis_size("gz") - 1
    make = functools.partial(Copy, send=send, recv=recv)

    barrier = pltpu.get_barrier_semaphore()
    for axis in AXES:
        for by in (1, -1):
            pl.semaphore_signal(
                barrier, inc=1, device_id={axis: around(axis, by)}, device_id_type=MESH
            )
    loads = [
        pltpu.make_async_copy(src, dst, local.at[k])
        for k, (src, dst) in enumerate(
            (
                (fields, fa.at[:, pl.ds(LOW, depth), own]),
                (material, mat.at[pl.ds(LOW, depth), own]),
                (profile, prof_a.at[own]),
                (forward, stored),
            )
        )
    ]
    for load in loads:
        load.start()
    pl.semaphore_wait(barrier, 2 * len(AXES))

    planes = [
        make(9, fields.at[pl.ds(0, 2), 0], fa.at[pl.ds(0, 2), top, own], "gz", -1),
        make(0, fields.at[:, depth - 1], fa.at[:, 1, own], "gz", 1),
        make(10, fields.at[pl.ds(2, 4), 0], fa.at[pl.ds(2, 4), top, own], "gz", -1),
        make(2, material.at[pl.ds(depth - 2, 2)], mat.at[pl.ds(0, 2), own], "gz", 1),
        make(12, material.at[0], mat.at[top, own], "gz", -1),
        make(1, fields.at[pl.ds(0, 5), depth - 2], fa.at[pl.ds(0, 5), 0, own], "gz", 1),
        make(11, fields.at[pl.ds(0, 2), 1], fa.at[pl.ds(0, 2), top + 1, own], "gz", -1),
    ]
    tiles = []
    for k, (by, edge) in enumerate(((-1, first), (1, final))):
        tiles += [
            make(19 + 4 * k, fields.at[:, :, edge], x_in.at[k], "gx", by),
            make(20 + 4 * k, material.at[:, edge], x_mat_in.at[k], "gx", by),
            make(21 + 4 * k, profile.at[edge], x_prof_in.at[k], "gx", by),
        ]
    for copy in tiles + planes:
        copy.start()

    lane = lax.broadcasted_iota(jnp.int32, (wide, lanes), 1)
    tile_row = lax.broadcasted_iota(jnp.int32, (8, lanes), 0)
    from_next = tile_row < HALO
    at_first, at_last = lane == 0, lane == lanes - 1

    for load in loads[:3]:
        load.wait()
    per = lanes // SLOT
    sources = [functools.partial(lambda c, p: fa[c, LOW + p, own], c, p) for c in range(6) for p in range(depth)]
    sources += [functools.partial(lambda p: mat[LOW + p, own].astype(jnp.float32), p) for p in range(depth)]
    sources += [lambda: prof_a[own]]
    slot_of = lane[:rows] // SLOT
    for half in range(2):
        filled = jnp.zeros((rows, lanes), jnp.float32)
        for s, read in enumerate(sources[half * per : (half + 1) * per]):
            filled = jnp.where(slot_of == s, pltpu.roll(read(), SLOT * s + HALO, 1), filled)
        packed[half] = filled
    columns = [make(27 + k, packed, y_in.at[k], "gy", by) for k, by in enumerate((-1, 1))]
    for copy in columns:
        copy.start()

    @pl.when(gz == 0)
    def _():
        fa[:, pl.ds(0, LOW)] = jnp.zeros((6, LOW, wide, lanes), jnp.float32)
        mat[pl.ds(0, LOW)] = jnp.zeros((LOW, wide, lanes), jnp.int32)
        z_border[0] = jnp.zeros(z_border.shape[1:], jnp.float32)
        for m in range(2):
            heard[m, 0] = jnp.zeros(heard.shape[2:], jnp.float32)

    @pl.when(gz == last)
    def _():
        fa[:, pl.ds(top, 2)] = jnp.zeros((6, 2, wide, lanes), jnp.float32)
        mat[top] = jnp.zeros((wide, lanes), jnp.int32)
        z_border[1] = jnp.zeros(z_border.shape[1:], jnp.float32)
        for m in range(2):
            heard[m, 1] = jnp.zeros(heard.shape[2:], jnp.float32)

    for copy in tiles:
        copy.arrived()
    for c in range(6):
        for p in range(depth):
            tile = jnp.where(from_next, x_in[0, c, p], x_in[1, c, p])
            x_out[c, p] = tile
            fa[c, LOW + p, extra] = tile
    for p in range(depth):
        tile = jnp.where(from_next, x_mat_in[0, p], x_mat_in[1, p])
        x_mat_out[p] = tile
        mat[LOW + p, extra] = tile
    prof_a[extra] = jnp.where(from_next, x_prof_in[0], x_prof_in[1])
    ghosts = [
        make(3, x_out.at[:, depth - 1], fa.at[:, 1, extra], "gz", 1),
        make(13, x_out.at[:, 0], fa.at[:, top, extra], "gz", -1),
        make(5, x_mat_out.at[pl.ds(depth - 2, 2)], mat.at[pl.ds(0, 2), extra], "gz", 1),
        make(15, x_mat_out.at[0], mat.at[top, extra], "gz", -1),
        make(4, x_out.at[pl.ds(0, 5), depth - 2], fa.at[pl.ds(0, 5), 0, extra], "gz", 1),
        make(14, x_out.at[pl.ds(0, 2), 1], fa.at[pl.ds(0, 2), top + 1, extra], "gz", -1),
    ]
    for copy in ghosts:
        copy.start()

    for copy in columns:
        copy.arrived()
    for half in range(2):
        border[half, own] = jnp.where(
            lane[:rows] % SLOT < HALO, y_in[1, half], y_in[0, half]
        )
    corners = [
        make(22 + 4 * k, border.at[:, edge], x_border_in.at[k], "gx", by)
        for k, (by, edge) in enumerate(((-1, first), (1, final)))
    ]
    for copy in corners:
        copy.start()

    table = [COURANT / jnp.full((1, lanes), eps_ref[m], jnp.float32) for m in range(eps_ref.shape[0])]

    def coef_a(p, keep=None):
        kinds = mat[p]
        value = jnp.broadcast_to(table[0], (wide, lanes))
        for m in range(1, len(table)):
            value = jnp.where(kinds == m, table[m], value)
        ca[p] = value if keep is None else value * keep

    def coef_b(p, kinds, keep=None):
        value = jnp.broadcast_to(table[0], kinds.shape)
        for m in range(1, len(table)):
            value = jnp.where(kinds > m - 0.5, table[m], value)
        cb[p] = value if keep is None else value * keep

    def unpack(ref, s):
        half, s = divmod(s, per)
        return pltpu.roll(ref[half], lanes - (SLOT * s + HALO), 1)

    run(LOW, top, coef_a)
    for copy in corners:
        copy.arrived()
    for half in range(2):
        border[half, extra] = jnp.where(from_next, x_border_in[0, half], x_border_in[1, half])
    borders = [
        make(6, border, z_border.at[0], "gz", 1),
        make(16, border, z_border.at[1], "gz", -1),
    ]
    for copy in borders:
        copy.start()

    for p in range(depth):
        for c in range(6):
            fb[c, LOW + p] = unpack(border, c * depth + p)
        coef_b(LOW + p, unpack(border, 6 * depth + p))
    prof_b[...] = unpack(border, 7 * depth)

    low_rate = COURANT * (gz != 0).astype(jnp.float32)

    def pair(c, p, t=0):
        if t > 0 and c < 2 and isinstance(p, int) and p in (0, top + 1):
            there = heard.at[t - 1, 0 if p == 0 else 1]
            return there[c], pltpu.roll(there[2], lanes // 2, 1) if c else there[2]
        return fa[c, p], fb[c, p]

    def minus(u, v):
        return u[0] - v[0], u[1] - v[1]

    def next_x(u):
        return tuple(pltpu.roll(v, wide - 1, 0) - v for v in u)

    def last_x(u):
        return tuple(v - pltpu.roll(v, 1, 0) for v in u)

    def next_y(u):
        a, b = (pltpu.roll(v, lanes - 1, 1) for v in u)
        return jnp.where(at_last, b, a) - u[0], jnp.where(at_last, a, b) - u[1]

    def last_y(u):
        a, b = (pltpu.roll(v, 1, 1) for v in u)
        return u[0] - jnp.where(at_first, b, a), u[1] - jnp.where(at_first, a, b)

    def put(c, p, value, t):
        fa[c, p], fb[c, p] = value
        if t == STEPS and not (isinstance(p, int) and not LOW <= p < top):
            out_ref[c, p - LOW] = value[0][:rows]

    def magnetic(p, t):
        low = isinstance(p, int) and p < LOW
        rate = low_rate if low else COURANT
        outer = isinstance(p, int) and p == 0

        def push(c, curl):
            old = fa[c, p], fb[c, p]
            put(c, p, tuple(o - rate * k for o, k in zip(old, curl)), t)

        ex, ey, ez = pair(0, p, t - 1), pair(1, p, t - 1), pair(2, p)
        push(3, minus(next_y(ez), minus(pair(1, p + 1, t - 1), ey)))
        push(4, minus(minus(pair(0, p + 1, t - 1), ex), next_x(ez)))
        if not outer:
            push(5, minus(next_x(ey), next_y(ex)))

    def electric(p, t):
        coef = ca[p], cb[p]

        def push(c, curl):
            old = fa[c, p], fb[c, p]
            put(c, p, tuple(o + k * d for o, k, d in zip(old, coef, curl)), t)

        hx, hy = pair(3, p), pair(4, p)
        push(2, minus(last_x(hy), last_y(hx)))
        if isinstance(p, int) and p == 0:
            return
        hz = pair(5, p)
        here = (gz * depth + p - LOW == plane_ref[0]).astype(jnp.float32)
        pushed = wave_ref[t - 1] * here
        curl = minus(last_y(hz), minus(hy, pair(4, p - 1)))
        push(0, (curl[0] + pushed * prof_a[...], curl[1] + pushed * prof_b[...]))
        push(1, minus(minus(hx, pair(3, p - 1)), last_x(hz)))

    def gather(p, t):
        total = jnp.zeros((rows, lanes), jnp.float32) if t == 1 else grad_ref[p - LOW]
        for c in range(3):
            total = total + stored[t - 1, c, p - LOW].astype(jnp.float32) * fa[c, p, own]
        if t == STEPS:
            total = jnp.where(mat[p, own] >= 2, -total, 0.0)
        grad_ref[p - LOW] = total

    def tell(t):
        copies = []
        for k, (p, by) in enumerate(((top - 2, 1), (LOW + 1, -1))):
            words = said.at[t - 1, k]
            words[0], words[1] = fa[0, p], fa[1, p]
            middle = (lane >= lanes // 4) & (lane < 3 * lanes // 4)
            words[2] = jnp.where(middle, pltpu.roll(fb[1, p], lanes // 2, 1), fb[0, p])
            copies.append(make(7 + 10 * k - 1 + t, words, heard.at[t - 1, k], "gz", by))
        for copy in copies:
            copy.start()
        return copies

    a, b = LOW, top - 1
    run(a, b, lambda p: magnetic(p, 1))
    run(a + 1, b, lambda p: electric(p, 1))
    first_told = tell(1)
    loads[3].wait()
    run(a + 1, b, lambda p: gather(p, 1))

    for copy in planes + ghosts + borders:
        copy.arrived()
    coef_a(1)
    for c in range(6):
        fb[c, 1] = unpack(z_border.at[0], c * depth + depth - 1)
    coef_b(1, unpack(z_border.at[0], 6 * depth + depth - 1))
    for c in range(6):
        fb[c, top] = unpack(z_border.at[1], c * depth)
    each((1, b), lambda p: magnetic(p, 1))
    each((a, b), lambda p: electric(p, 1))
    run(a, b, lambda p: magnetic(p, 2))
    each((a, b), lambda p: gather(p, 1))
    run(a + 1, b, lambda p: electric(p, 2))
    second_told = tell(2)
    run(a + 1, b, lambda p: gather(p, 2))

    keep = (gz != last).astype(jnp.float32)
    coef_a(0)
    coef_a(top, keep)
    for c in range(5):
        fb[c, 0] = unpack(z_border.at[0], c * depth + depth - 2)
    coef_b(0, unpack(z_border.at[0], 6 * depth + depth - 2))
    coef_b(top, unpack(z_border.at[1], 6 * depth), keep)
    for c in range(2):
        fb[c, top + 1] = unpack(z_border.at[1], c * depth + 1)
    each((0, top), lambda p: magnetic(p, 1))
    each((0, 1, top), lambda p: electric(p, 1))
    each((1, b), lambda p: magnetic(p, 2))
    each((a, b), lambda p: electric(p, 2))
    each((a, b), lambda p: gather(p, 2))
    run(a, b, lambda p: magnetic(p, 3))
    run(a + 1, b, lambda p: electric(p, 3))
    run(a + 1, b, lambda p: gather(p, 3))
    magnetic(a + 1, 4)

    for copy in first_told:
        copy.arrived()
    each((0, top), lambda p: magnetic(p, 2))
    each((0, 1, top), lambda p: electric(p, 2))
    each((1, b), lambda p: magnetic(p, 3))
    each((a, b), lambda p: electric(p, 3))
    each((a, b), lambda p: gather(p, 3))
    each((a, b - 1), lambda p: magnetic(p, 4))
    each((a + 1, b - 1), lambda p: electric(p, 4))
    each((a + 1, b - 1), lambda p: gather(p, 4))

    for copy in second_told:
        copy.arrived()
    each((0, top), lambda p: magnetic(p, 3))
    each((1, top), lambda p: electric(p, 3))
    each((1, b), lambda p: magnetic(p, 4))
    each((a, b), lambda p: electric(p, 4))
    each((a, b), lambda p: gather(p, 4))

    for copy in planes + tiles + columns + ghosts + corners + borders + first_told + second_told:
        copy.sent()


def on_device(
    fields_in, material, material_eps, source_plane, source_wave, source_profile, forward_fields
):
    depth, rows, lanes = material.shape
    wide = rows + 2 * HALO
    levels = depth + 2 * LOW
    f32 = jnp.float32
    whole = pl.BlockSpec(memory_space=pltpu.VMEM)
    scalars = pl.BlockSpec(memory_space=pltpu.SMEM)
    remote = pl.BlockSpec(memory_space=pltpu.HBM)
    return pl.pallas_call(
        kernel,
        out_shape=(
            jax.ShapeDtypeStruct(fields_in.shape, f32),
            jax.ShapeDtypeStruct(material.shape, f32),
        ),
        in_specs=[scalars] * 3 + [remote] * 4,
        out_specs=(whole, whole),
        scratch_shapes=[
            pltpu.VMEM((6, levels, wide, lanes), f32),
            pltpu.VMEM((6, levels, wide, lanes), f32),
            pltpu.VMEM((levels, wide, lanes), f32),
            pltpu.VMEM((levels, wide, lanes), f32),
            pltpu.VMEM((levels, wide, lanes), jnp.int32),
            pltpu.VMEM((wide, lanes), f32),
            pltpu.VMEM((wide, lanes), f32),
            pltpu.VMEM(forward_fields.shape, forward_fields.dtype),
            pltpu.VMEM((2, rows, lanes), f32),
            pltpu.VMEM((2, 2, rows, lanes), f32),
            pltpu.VMEM((2, wide, lanes), f32),
            pltpu.VMEM((2, 2, wide, lanes), f32),
            pltpu.VMEM((2, 6, depth, 8, lanes), f32),
            pltpu.VMEM((2, depth, 8, lanes), jnp.int32),
            pltpu.VMEM((2, 8, lanes), f32),
            pltpu.VMEM((2, 2, 8, lanes), f32),
            pltpu.VMEM((6, depth, 8, lanes), f32),
            pltpu.VMEM((depth, 8, lanes), jnp.int32),
            pltpu.VMEM((2, 2, 3, wide, lanes), f32),
            pltpu.VMEM((2, 2, 3, wide, lanes), f32),
            pltpu.SemaphoreType.DMA((4,)),
            pltpu.SemaphoreType.DMA((COPIES,)),
            pltpu.SemaphoreType.DMA((COPIES,)),
        ],
        compiler_params=pltpu.CompilerParams(
            collective_id=0, has_side_effects=True, vmem_limit_bytes=40 << 20
        ),
    )(
        material_eps,
        source_plane,
        source_wave,
        fields_in,
        material,
        source_profile,
        forward_fields,
    )


def solution(mesh):
    placed = (
        P(None, "gz", "gx", "gy"),
        P("gz", "gx", "gy"),
        P(),
        P(),
        P(),
        P("gx", "gy"),
        P(None, None, "gz", "gx", "gy"),
    )
    return jax.shard_map(
        on_device,
        mesh=mesh,
        in_specs=placed,
        out_specs=(P(None, "gz", "gx", "gy"), P("gz", "gx", "gy")),
        check_vma=False,
    )
```

```python
import functools

import jax
import jax.numpy as jnp
from jax import lax
from jax.experimental import pallas as pl
from jax.experimental.pallas import tpu as pltpu
from jax.sharding import PartitionSpec as P

COURANT = 0.5
MESH = pl.DeviceIdType.MESH
STEPS = 4
LOW = 2
HALO = 4
SLOT = 2 * HALO
COPIES = 31


def around(axis, by):
    size = lax.axis_size(axis)
    return lax.rem(lax.axis_index(axis) + by + size, size)


class Copy:
    def __init__(self, k, src, dst, send, recv, **steps):
        self.end = "gz" in steps
        by = steps.get("gz", 1)
        last = lax.axis_size("gz") - 1
        self.sends = lax.axis_index("gz") != (last if by > 0 else 0)
        self.takes = lax.axis_index("gz") != (0 if by > 0 else last)
        self.copy = pltpu.make_async_remote_copy(
            src_ref=src,
            dst_ref=dst,
            send_sem=send.at[k],
            recv_sem=recv.at[k],
            device_id={axis: around(axis, n) for axis, n in steps.items()},
            device_id_type=MESH,
        )

    def _on(self, flag, act):
        if self.end:
            pl.when(flag)(act)
        else:
            act()

    def start(self):
        self._on(self.sends, self.copy.start)

    def sent(self):
        self._on(self.sends, self.copy.wait_send)

    def arrived(self):
        self._on(self.takes, self.copy.wait_recv)


def each(planes, act):
    for p in planes:
        act(p)


def run(lo, hi, act):
    if hi - lo == 1:
        act(lo)
    else:
        lax.fori_loop(lo, hi, lambda p, _: (act(p), 0)[1], 0)


def kernel(
    eps_ref,
    plane_ref,
    wave_ref,
    fields,
    material,
    profile,
    forward,
    out_ref,
    grad_ref,
    fa,
    fb,
    ca,
    cb,
    mat,
    prof_a,
    prof_b,
    stored,
    packed,
    y_in,
    border,
    z_border,
    x_pack,
    x_mat_pack,
    x_in,
    x_mat_in,
    x_prof_in,
    x_border_in,
    x_out,
    x_mat_out,
    said,
    heard,
    local,
    send,
    recv,
):
    _, depth, rows, lanes = fields.shape
    wide = rows + 2 * HALO
    own = pl.ds(0, rows)
    extra = pl.ds(rows, 2 * HALO)
    first, final = pl.ds(0, 8), pl.ds(rows - 8, 8)
    top = LOW + depth
    gz, last = lax.axis_index("gz"), lax.axis_size("gz") - 1
    make = functools.partial(Copy, send=send, recv=recv)

    barrier = pltpu.get_barrier_semaphore()

    def greet(**steps):
        there = {axis: around(axis, n) for axis, n in steps.items()}
        pl.semaphore_signal(barrier, inc=1, device_id=there, device_id_type=MESH)

    pl.when(gz != last)(lambda: greet(gz=1))
    pl.when(gz != 0)(lambda: greet(gz=-1))
    for by in (1, -1):
        greet(gx=by)
        greet(gy=by)
        for n in (1, -1):
            greet(gx=by, gy=n)
    loads = [
        pltpu.make_async_copy(src, dst, local.at[k])
        for k, (src, dst) in enumerate(
            (
                (fields, fa.at[:, pl.ds(LOW, depth), own]),
                (material, mat.at[pl.ds(LOW, depth), own]),
                (profile, prof_a.at[own]),
                (forward, stored),
            )
        )
    ]
    for load in loads:
        load.start()
    edge = (gz == 0) | (gz == last)
    pl.semaphore_wait(barrier, jnp.where(edge, 9, 10))

    falling = [
        make(9, fields.at[:, 0], fa.at[:, top, own], gz=-1),
        make(12, material.at[0], mat.at[top, own], gz=-1),
    ]
    rising = [
        make(0, fields.at[:, depth - 1], fa.at[:, 1, own], gz=1),
        make(2, material.at[pl.ds(depth - 2, 2)], mat.at[pl.ds(0, 2), own], gz=1),
    ]
    outer = [
        make(1, fields.at[pl.ds(0, 5), depth - 2], fa.at[pl.ds(0, 5), 0, own], gz=1),
        make(11, fields.at[pl.ds(0, 2), 1], fa.at[pl.ds(0, 2), top + 1, own], gz=-1),
    ]
    planes = falling + rising
    for copy in falling + rising:
        copy.start()

    lane = lax.broadcasted_iota(jnp.int32, (wide, lanes), 1)
    tile_row = lax.broadcasted_iota(jnp.int32, (8, lanes), 0)
    from_next = tile_row < HALO
    at_first, at_last = lane == 0, lane == lanes - 1

    for load in loads[:3]:
        load.wait()

    def turned(tile):
        return pltpu.roll(tile, HALO, 0)

    tiles = []
    for k, (by, edge) in enumerate(((-1, first), (1, final))):
        for h in range(depth // 2):
            p = LOW + 2 * h
            for source, dest in [(fa.at[c], x_pack.at[k, c, h]) for c in range(6)] + [
                (mat, x_mat_pack.at[k, h])
            ]:
                one, two = source[p, edge], source[p + 1, edge]
                one, two = (one, turned(two)) if k == 0 else (turned(one), two)
                dest[...] = jnp.where(from_next, one, two)
        tiles += [
            make(19 + 3 * k, x_pack.at[k], x_in.at[k], gx=by),
            make(20 + 3 * k, x_mat_pack.at[k], x_mat_in.at[k], gx=by),
            make(21 + 3 * k, profile.at[edge], x_prof_in.at[k], gx=by),
        ]
    for copy in tiles:
        copy.start()

    def narrow(c, p):
        return mat[LOW + p, own].astype(jnp.float32) if c == 6 else fa[c, LOW + p, own]

    def place(c, p):
        return p // 2, 7 * (p % 2) + c

    profile_place = (0, 14)
    slot_of = lane[:rows] // SLOT
    for half in range(2):
        filled = jnp.zeros((rows, lanes), jnp.float32)
        pieces = [(place(c, p)[1], narrow(c, p)) for p in (2 * half, 2 * half + 1) for c in range(7)]
        if half == profile_place[0]:
            pieces.append((profile_place[1], prof_a[own]))
        for s, value in pieces:
            filled = jnp.where(slot_of == s, pltpu.roll(value, SLOT * s + HALO, 1), filled)
        packed[half] = filled
    columns = [make(29 + k, packed, y_in.at[k], gy=by) for k, by in enumerate((-1, 1))]
    corners = [
        make(25 + 2 * k + n, packed.at[:, edge], x_border_in.at[k, n], gx=by, gy=way)
        for k, (by, edge) in enumerate(((-1, first), (1, final)))
        for n, way in enumerate((-1, 1))
    ]
    for copy in corners + columns:
        copy.start()

    @pl.when(gz == 0)
    def _():
        fa[:, pl.ds(0, LOW)] = jnp.zeros((6, LOW, wide, lanes), jnp.float32)
        mat[pl.ds(0, LOW)] = jnp.zeros((LOW, wide, lanes), jnp.int32)
        z_border[0] = jnp.zeros(z_border.shape[1:], jnp.float32)
        for m in range(2):
            heard[m, 0] = jnp.zeros(heard.shape[2:], jnp.float32)

    @pl.when(gz == last)
    def _():
        fa[:, pl.ds(top, 2)] = jnp.zeros((6, 2, wide, lanes), jnp.float32)
        mat[top] = jnp.zeros((wide, lanes), jnp.int32)
        z_border[1] = jnp.zeros(z_border.shape[1:], jnp.float32)
        for m in range(2):
            heard[m, 1] = jnp.zeros(heard.shape[2:], jnp.float32)

    for copy in tiles:
        copy.arrived()

    def meet(after, before, p):
        after, before = (turned(after), before) if p % 2 else (after, turned(before))
        return jnp.where(from_next, after, before)

    for c in range(6):
        for p in range(depth):
            tile = meet(x_in[0, c, p // 2], x_in[1, c, p // 2], p)
            x_out[c, p] = tile
            fa[c, LOW + p, extra] = tile
    for p in range(depth):
        tile = meet(x_mat_in[0, p // 2], x_mat_in[1, p // 2], p)
        x_mat_out[p] = tile
        mat[LOW + p, extra] = tile
    prof_a[extra] = jnp.where(from_next, x_prof_in[0], x_prof_in[1])
    ghosts = [
        make(13, x_out.at[:, 0], fa.at[:, top, extra], gz=-1),
        make(15, x_mat_out.at[0], mat.at[top, extra], gz=-1),
        make(3, x_out.at[:, depth - 1], fa.at[:, 1, extra], gz=1),
        make(5, x_mat_out.at[pl.ds(depth - 2, 2)], mat.at[pl.ds(0, 2), extra], gz=1),
    ]
    outer += [
        make(4, x_out.at[pl.ds(0, 5), depth - 2], fa.at[pl.ds(0, 5), 0, extra], gz=1),
        make(14, x_out.at[pl.ds(0, 2), 1], fa.at[pl.ds(0, 2), top + 1, extra], gz=-1),
    ]
    for copy in ghosts:
        copy.start()

    for copy in columns:
        copy.arrived()
    from_below = lane % SLOT < HALO
    for half in range(2):
        border[half, own] = jnp.where(from_below[:rows], y_in[1, half], y_in[0, half])
    table = [COURANT / jnp.full((1, lanes), eps_ref[m], jnp.float32) for m in range(eps_ref.shape[0])]

    def coef_a(p, keep=None):
        kinds = mat[p]
        value = jnp.broadcast_to(table[0], (wide, lanes))
        for m in range(1, len(table)):
            value = jnp.where(kinds == m, table[m], value)
        ca[p] = value if keep is None else value * keep

    def coef_b(p, kinds, keep=None):
        value = jnp.broadcast_to(table[0], kinds.shape)
        for m in range(1, len(table)):
            value = jnp.where(kinds > m - 0.5, table[m], value)
        cb[p] = value if keep is None else value * keep

    def unpack(value, s):
        return pltpu.roll(value, lanes - (SLOT * s + HALO), 1)

    run(LOW, top, coef_a)
    for copy in corners:
        copy.arrived()
    for half in range(2):
        tile = jnp.where(from_next, x_border_in[0, :, half], x_border_in[1, :, half])
        border[half, extra] = jnp.where(from_below[:8], tile[1], tile[0])
    borders = [
        make(6, border.at[1], z_border.at[0], gz=1),
        make(16, border.at[0], z_border.at[1], gz=-1),
    ]
    for copy in borders + outer:
        copy.start()

    for p in range(depth):
        for c in range(6):
            fb[c, LOW + p] = unpack(border[place(c, p)[0]], place(c, p)[1])
        coef_b(LOW + p, unpack(border[place(6, p)[0]], place(6, p)[1]))
    prof_b[...] = unpack(border[profile_place[0]], profile_place[1])

    low_rate = COURANT * (gz != 0).astype(jnp.float32)

    def pair(c, p, t=0):
        if t > 0 and c < 2 and isinstance(p, int) and p in (0, top + 1):
            there = heard.at[t - 1, 0 if p == 0 else 1]
            return there[c], pltpu.roll(there[2], lanes // 2, 1) if c else there[2]
        return fa[c, p], fb[c, p]

    def minus(u, v):
        return u[0] - v[0], u[1] - v[1]

    def next_x(u):
        return tuple(pltpu.roll(v, wide - 1, 0) - v for v in u)

    def last_x(u):
        return tuple(v - pltpu.roll(v, 1, 0) for v in u)

    def next_y(u):
        a, b = (pltpu.roll(v, lanes - 1, 1) for v in u)
        return jnp.where(at_last, b, a) - u[0], jnp.where(at_last, a, b) - u[1]

    def last_y(u):
        a, b = (pltpu.roll(v, 1, 1) for v in u)
        return u[0] - jnp.where(at_first, b, a), u[1] - jnp.where(at_first, a, b)

    def put(c, p, value, t):
        fa[c, p], fb[c, p] = value
        if t == STEPS and not (isinstance(p, int) and not LOW <= p < top):
            out_ref[c, p - LOW] = value[0][:rows]

    def magnetic(p, t):
        low = isinstance(p, int) and p < LOW
        rate = low_rate if low else COURANT
        outer = isinstance(p, int) and p == 0

        def push(c, curl):
            old = fa[c, p], fb[c, p]
            put(c, p, tuple(o - rate * k for o, k in zip(old, curl)), t)

        ex, ey, ez = pair(0, p, t - 1), pair(1, p, t - 1), pair(2, p)
        push(3, minus(next_y(ez), minus(pair(1, p + 1, t - 1), ey)))
        push(4, minus(minus(pair(0, p + 1, t - 1), ex), next_x(ez)))
        if not outer:
            push(5, minus(next_x(ey), next_y(ex)))

    def electric(p, t):
        coef = ca[p], cb[p]

        def push(c, curl):
            old = fa[c, p], fb[c, p]
            put(c, p, tuple(o + k * d for o, k, d in zip(old, coef, curl)), t)

        hx, hy = pair(3, p), pair(4, p)
        push(2, minus(last_x(hy), last_y(hx)))
        if isinstance(p, int) and p == 0:
            return
        hz = pair(5, p)
        here = (gz * depth + p - LOW == plane_ref[0]).astype(jnp.float32)
        pushed = wave_ref[t - 1] * here
        curl = minus(last_y(hz), minus(hy, pair(4, p - 1)))
        push(0, (curl[0] + pushed * prof_a[...], curl[1] + pushed * prof_b[...]))
        push(1, minus(minus(hx, pair(3, p - 1)), last_x(hz)))

    def gather(p, t):
        total = jnp.zeros((rows, lanes), jnp.float32) if t == 1 else grad_ref[p - LOW]
        for c in range(3):
            total = total + stored[t - 1, c, p - LOW].astype(jnp.float32) * fa[c, p, own]
        if t == STEPS:
            total = jnp.where(mat[p, own] >= 2, -total, 0.0)
        grad_ref[p - LOW] = total

    def tell(t):
        copies = []
        for k, (p, by) in enumerate(((top - 2, 1), (LOW + 1, -1))):
            words = said.at[t - 1, k]
            words[0], words[1] = fa[0, p], fa[1, p]
            middle = (lane >= lanes // 4) & (lane < 3 * lanes // 4)
            words[2] = jnp.where(middle, pltpu.roll(fb[1, p], lanes // 2, 1), fb[0, p])
            copies.append(make(7 + 10 * k - 1 + t, words, heard.at[t - 1, k], gz=by))
        for copy in copies:
            copy.start()
        return copies

    a, b = LOW, top - 1
    run(a, b, lambda p: magnetic(p, 1))
    run(a + 1, b, lambda p: electric(p, 1))
    first_told = tell(1)
    loads[3].wait()
    run(a + 1, b, lambda p: gather(p, 1))

    for copy in planes + ghosts + borders:
        copy.arrived()
    coef_a(1)
    for c in range(6):
        fb[c, 1] = unpack(z_border[0], place(c, depth - 1)[1])
    coef_b(1, unpack(z_border[0], place(6, depth - 1)[1]))
    for c in range(6):
        fb[c, top] = unpack(z_border[1], place(c, 0)[1])
    each((1, b), lambda p: magnetic(p, 1))
    each((a, b), lambda p: electric(p, 1))
    run(a, b, lambda p: magnetic(p, 2))
    each((a, b), lambda p: gather(p, 1))
    run(a + 1, b, lambda p: electric(p, 2))
    second_told = tell(2)
    run(a + 1, b, lambda p: gather(p, 2))

    for copy in outer:
        copy.arrived()
    keep = (gz != last).astype(jnp.float32)
    coef_a(0)
    coef_a(top, keep)
    for c in range(5):
        fb[c, 0] = unpack(z_border[0], place(c, depth - 2)[1])
    coef_b(0, unpack(z_border[0], place(6, depth - 2)[1]))
    coef_b(top, unpack(z_border[1], place(6, 0)[1]), keep)
    for c in range(2):
        fb[c, top + 1] = unpack(z_border[1], place(c, 1)[1])
    each((0, top), lambda p: magnetic(p, 1))
    each((0, 1, top), lambda p: electric(p, 1))
    each((1, b), lambda p: magnetic(p, 2))
    each((a, b), lambda p: electric(p, 2))
    each((a, b), lambda p: gather(p, 2))
    run(a, b, lambda p: magnetic(p, 3))
    run(a + 1, b, lambda p: electric(p, 3))
    run(a + 1, b, lambda p: gather(p, 3))
    magnetic(a + 1, 4)

    for copy in first_told:
        copy.arrived()
    each((0, top), lambda p: magnetic(p, 2))
    each((0, 1, top), lambda p: electric(p, 2))
    each((1, b), lambda p: magnetic(p, 3))
    each((a, b), lambda p: electric(p, 3))
    each((a, b), lambda p: gather(p, 3))
    each((a, b - 1), lambda p: magnetic(p, 4))
    each((a + 1, b - 1), lambda p: electric(p, 4))
    each((a + 1, b - 1), lambda p: gather(p, 4))

    for copy in second_told:
        copy.arrived()
    each((0, top), lambda p: magnetic(p, 3))
    each((1, top), lambda p: electric(p, 3))
    each((1, b), lambda p: magnetic(p, 4))
    each((a, b), lambda p: electric(p, 4))
    each((a, b), lambda p: gather(p, 4))

    for copy in planes + outer + tiles + columns + ghosts + corners + borders + first_told + second_told:
        copy.sent()


def on_device(
    fields_in, material, material_eps, source_plane, source_wave, source_profile, forward_fields
):
    depth, rows, lanes = material.shape
    wide = rows + 2 * HALO
    levels = depth + 2 * LOW
    f32 = jnp.float32
    whole = pl.BlockSpec(memory_space=pltpu.VMEM)
    scalars = pl.BlockSpec(memory_space=pltpu.SMEM)
    remote = pl.BlockSpec(memory_space=pltpu.HBM)
    return pl.pallas_call(
        kernel,
        out_shape=(
            jax.ShapeDtypeStruct(fields_in.shape, f32),
            jax.ShapeDtypeStruct(material.shape, f32),
        ),
        in_specs=[scalars] * 3 + [remote] * 4,
        out_specs=(whole, whole),
        scratch_shapes=[
            pltpu.VMEM((6, levels, wide, lanes), f32),
            pltpu.VMEM((6, levels, wide, lanes), f32),
            pltpu.VMEM((levels, wide, lanes), f32),
            pltpu.VMEM((levels, wide, lanes), f32),
            pltpu.VMEM((levels, wide, lanes), jnp.int32),
            pltpu.VMEM((wide, lanes), f32),
            pltpu.VMEM((wide, lanes), f32),
            pltpu.VMEM(forward_fields.shape, forward_fields.dtype),
            pltpu.VMEM((2, rows, lanes), f32),
            pltpu.VMEM((2, 2, rows, lanes), f32),
            pltpu.VMEM((2, wide, lanes), f32),
            pltpu.VMEM((2, wide, lanes), f32),
            pltpu.VMEM((2, 6, depth // 2, 8, lanes), f32),
            pltpu.VMEM((2, depth // 2, 8, lanes), jnp.int32),
            pltpu.VMEM((2, 6, depth // 2, 8, lanes), f32),
            pltpu.VMEM((2, depth // 2, 8, lanes), jnp.int32),
            pltpu.VMEM((2, 8, lanes), f32),
            pltpu.VMEM((2, 2, 2, 8, lanes), f32),
            pltpu.VMEM((6, depth, 8, lanes), f32),
            pltpu.VMEM((depth, 8, lanes), jnp.int32),
            pltpu.VMEM((2, 2, 3, wide, lanes), f32),
            pltpu.VMEM((2, 2, 3, wide, lanes), f32),
            pltpu.SemaphoreType.DMA((4,)),
            pltpu.SemaphoreType.DMA((COPIES,)),
            pltpu.SemaphoreType.DMA((COPIES,)),
        ],
        compiler_params=pltpu.CompilerParams(
            collective_id=0, has_side_effects=True, vmem_limit_bytes=60 << 20
        ),
    )(
        material_eps,
        source_plane,
        source_wave,
        fields_in,
        material,
        source_profile,
        forward_fields,
    )


def solution(mesh):
    placed = (
        P(None, "gz", "gx", "gy"),
        P("gz", "gx", "gy"),
        P(),
        P(),
        P(),
        P("gx", "gy"),
        P(None, None, "gz", "gx", "gy"),
    )
    return jax.shard_map(
        on_device,
        mesh=mesh,
        in_specs=placed,
        out_specs=(P(None, "gz", "gx", "gy"), P("gz", "gx", "gy")),
        check_vma=False,
    )
```

```python
import functools

import jax
import jax.numpy as jnp
from jax import lax
from jax.experimental import pallas as pl
from jax.experimental.pallas import tpu as pltpu
from jax.sharding import PartitionSpec as P

COURANT = 0.5
MESH = pl.DeviceIdType.MESH
STEPS = 4
LOW = 2
HALO = 4
SLOT = 2 * HALO
COPIES = 31
CHIPS_Z = 16


def around(axis, by):
    size = lax.axis_size(axis)
    return lax.rem(lax.axis_index(axis) + by + size, size)


class Copy:
    def __init__(self, k, src, dst, send, recv, **steps):
        self.end = "gz" in steps
        by = steps.get("gz", 1)
        last = lax.axis_size("gz") - 1
        self.sends = lax.axis_index("gz") != (last if by > 0 else 0)
        self.takes = lax.axis_index("gz") != (0 if by > 0 else last)
        self.copy = pltpu.make_async_remote_copy(
            src_ref=src,
            dst_ref=dst,
            send_sem=send.at[k],
            recv_sem=recv.at[k],
            device_id={axis: around(axis, n) for axis, n in steps.items()},
            device_id_type=MESH,
        )

    def _on(self, flag, act):
        if self.end:
            pl.when(flag)(act)
        else:
            act()

    def start(self):
        self._on(self.sends, self.copy.start)

    def sent(self):
        self._on(self.sends, self.copy.wait_send)

    def arrived(self):
        self._on(self.takes, self.copy.wait_recv)


def each(planes, act):
    for p in planes:
        act(p)


def run(lo, hi, act):
    if hi - lo == 1:
        act(lo)
    else:
        lax.fori_loop(lo, hi, lambda p, _: (act(p), 0)[1], 0)


def kernel(
    eps_ref,
    plane_ref,
    wave_ref,
    fields,
    material,
    profile,
    forward,
    out_ref,
    grad_ref,
    fa,
    fb,
    ca,
    cb,
    mat,
    prof_a,
    prof_b,
    stored,
    packed,
    y_in,
    border,
    z_border,
    x_pack,
    x_mat_pack,
    x_in,
    x_mat_in,
    x_prof_in,
    x_border_in,
    x_out,
    x_mat_out,
    said,
    heard,
    local,
    send,
    recv,
):
    _, depth, rows, lanes = fields.shape
    wide = rows + 2 * HALO
    own = pl.ds(0, rows)
    extra = pl.ds(rows, 2 * HALO)
    first, final = pl.ds(0, 8), pl.ds(rows - 8, 8)
    top = LOW + depth
    gz, last = lax.axis_index("gz"), lax.axis_size("gz") - 1
    make = functools.partial(Copy, send=send, recv=recv)

    barrier = pltpu.get_barrier_semaphore()

    def greet(**steps):
        there = {axis: around(axis, n) for axis, n in steps.items()}
        pl.semaphore_signal(barrier, inc=1, device_id=there, device_id_type=MESH)

    pl.when(gz != last)(lambda: greet(gz=1))
    pl.when(gz != 0)(lambda: greet(gz=-1))
    for by in (1, -1):
        greet(gx=by)
        greet(gy=by)
        for n in (1, -1):
            greet(gx=by, gy=n)
    loads = [
        pltpu.make_async_copy(src, dst, local.at[k])
        for k, (src, dst) in enumerate(
            (
                (fields, fa.at[:, pl.ds(LOW, depth), own]),
                (material, mat.at[pl.ds(LOW, depth), own]),
                (profile, prof_a.at[own]),
                (forward, stored),
            )
        )
    ]
    for load in loads:
        load.start()
    edge = (gz == 0) | (gz == last)
    pl.semaphore_wait(barrier, jnp.where(edge, 9, 10))

    falling = [
        make(9, fields.at[:, 0], fa.at[:, top, own], gz=-1),
        make(12, material.at[0], mat.at[top, own], gz=-1),
    ]
    rising = [
        make(0, fields.at[:, depth - 1], fa.at[:, 1, own], gz=1),
        make(2, material.at[pl.ds(depth - 2, 2)], mat.at[pl.ds(0, 2), own], gz=1),
    ]
    outer = [
        make(1, fields.at[pl.ds(0, 5), depth - 2], fa.at[pl.ds(0, 5), 0, own], gz=1),
        make(11, fields.at[pl.ds(0, 2), 1], fa.at[pl.ds(0, 2), top + 1, own], gz=-1),
    ]
    planes = falling + rising
    turn = gz % CHIPS_Z == 0
    for copy in rising:
        copy.start()

    @pl.when(~turn)
    def _():
        for copy in falling:
            copy.start()

    lane = lax.broadcasted_iota(jnp.int32, (wide, lanes), 1)
    tile_row = lax.broadcasted_iota(jnp.int32, (8, lanes), 0)
    from_next = tile_row < HALO
    at_first, at_last = lane == 0, lane == lanes - 1

    for load in loads[:3]:
        load.wait()

    def turned(tile):
        return pltpu.roll(tile, HALO, 0)

    tiles = []
    for k, (by, edge) in enumerate(((-1, first), (1, final))):
        for h in range(depth // 2):
            p = LOW + 2 * h
            for source, dest in [(fa.at[c], x_pack.at[k, c, h]) for c in range(6)] + [
                (mat, x_mat_pack.at[k, h])
            ]:
                one, two = source[p, edge], source[p + 1, edge]
                one, two = (one, turned(two)) if k == 0 else (turned(one), two)
                dest[...] = jnp.where(from_next, one, two)
        tiles += [
            make(19 + 3 * k, x_pack.at[k], x_in.at[k], gx=by),
            make(20 + 3 * k, x_mat_pack.at[k], x_mat_in.at[k], gx=by),
            make(21 + 3 * k, profile.at[edge], x_prof_in.at[k], gx=by),
        ]
    for copy in tiles:
        copy.start()

    def narrow(c, p):
        return mat[LOW + p, own].astype(jnp.float32) if c == 6 else fa[c, LOW + p, own]

    def place(c, p):
        return p // 2, 7 * (p % 2) + c

    profile_place = (0, 14)
    slot_of = lane[:rows] // SLOT
    for half in range(2):
        filled = jnp.zeros((rows, lanes), jnp.float32)
        pieces = [(place(c, p)[1], narrow(c, p)) for p in (2 * half, 2 * half + 1) for c in range(7)]
        if half == profile_place[0]:
            pieces.append((profile_place[1], prof_a[own]))
        for s, value in pieces:
            filled = jnp.where(slot_of == s, pltpu.roll(value, SLOT * s + HALO, 1), filled)
        packed[half] = filled
    columns = [make(29 + k, packed, y_in.at[k], gy=by) for k, by in enumerate((-1, 1))]
    corners = [
        make(25 + 2 * k + n, packed.at[:, edge], x_border_in.at[k, n], gx=by, gy=way)
        for k, (by, edge) in enumerate(((-1, first), (1, final)))
        for n, way in enumerate((-1, 1))
    ]
    for copy in corners + columns:
        copy.start()

    @pl.when(gz == 0)
    def _():
        fa[:, pl.ds(0, LOW)] = jnp.zeros((6, LOW, wide, lanes), jnp.float32)
        mat[pl.ds(0, LOW)] = jnp.zeros((LOW, wide, lanes), jnp.int32)
        z_border[0] = jnp.zeros(z_border.shape[1:], jnp.float32)
        for m in range(2):
            heard[m, 0] = jnp.zeros(heard.shape[2:], jnp.float32)

    @pl.when(gz == last)
    def _():
        fa[:, pl.ds(top, 2)] = jnp.zeros((6, 2, wide, lanes), jnp.float32)
        mat[top] = jnp.zeros((wide, lanes), jnp.int32)
        z_border[1] = jnp.zeros(z_border.shape[1:], jnp.float32)
        for m in range(2):
            heard[m, 1] = jnp.zeros(heard.shape[2:], jnp.float32)

    for copy in tiles:
        copy.arrived()

    @pl.when(turn)
    def _():
        for copy in falling:
            copy.start()

    def meet(after, before, p):
        after, before = (turned(after), before) if p % 2 else (after, turned(before))
        return jnp.where(from_next, after, before)

    for c in range(6):
        for p in range(depth):
            tile = meet(x_in[0, c, p // 2], x_in[1, c, p // 2], p)
            x_out[c, p] = tile
            fa[c, LOW + p, extra] = tile
    for p in range(depth):
        tile = meet(x_mat_in[0, p // 2], x_mat_in[1, p // 2], p)
        x_mat_out[p] = tile
        mat[LOW + p, extra] = tile
    prof_a[extra] = jnp.where(from_next, x_prof_in[0], x_prof_in[1])
    ghosts = [
        make(13, x_out.at[:, 0], fa.at[:, top, extra], gz=-1),
        make(15, x_mat_out.at[0], mat.at[top, extra], gz=-1),
        make(3, x_out.at[:, depth - 1], fa.at[:, 1, extra], gz=1),
        make(5, x_mat_out.at[pl.ds(depth - 2, 2)], mat.at[pl.ds(0, 2), extra], gz=1),
    ]
    outer += [
        make(4, x_out.at[pl.ds(0, 5), depth - 2], fa.at[pl.ds(0, 5), 0, extra], gz=1),
        make(14, x_out.at[pl.ds(0, 2), 1], fa.at[pl.ds(0, 2), top + 1, extra], gz=-1),
    ]
    for copy in ghosts:
        copy.start()

    for copy in columns:
        copy.arrived()
    from_below = lane % SLOT < HALO
    for half in range(2):
        border[half, own] = jnp.where(from_below[:rows], y_in[1, half], y_in[0, half])
    table = [COURANT / jnp.full((1, lanes), eps_ref[m], jnp.float32) for m in range(eps_ref.shape[0])]

    def coef_a(p, keep=None):
        kinds = mat[p]
        value = jnp.broadcast_to(table[0], (wide, lanes))
        for m in range(1, len(table)):
            value = jnp.where(kinds == m, table[m], value)
        ca[p] = value if keep is None else value * keep

    def coef_b(p, kinds, keep=None):
        value = jnp.broadcast_to(table[0], kinds.shape)
        for m in range(1, len(table)):
            value = jnp.where(kinds > m - 0.5, table[m], value)
        cb[p] = value if keep is None else value * keep

    def unpack(value, s):
        return pltpu.roll(value, lanes - (SLOT * s + HALO), 1)

    run(LOW, top, coef_a)
    for copy in corners:
        copy.arrived()
    for half in range(2):
        tile = jnp.where(from_next, x_border_in[0, :, half], x_border_in[1, :, half])
        border[half, extra] = jnp.where(from_below[:8], tile[1], tile[0])
    borders = [
        make(6, border.at[1], z_border.at[0], gz=1),
        make(16, border.at[0], z_border.at[1], gz=-1),
    ]
    for copy in borders + outer:
        copy.start()

    for p in range(depth):
        for c in range(6):
            fb[c, LOW + p] = unpack(border[place(c, p)[0]], place(c, p)[1])
        coef_b(LOW + p, unpack(border[place(6, p)[0]], place(6, p)[1]))
    prof_b[...] = unpack(border[profile_place[0]], profile_place[1])

    low_rate = COURANT * (gz != 0).astype(jnp.float32)

    def pair(c, p, t=0):
        if t > 0 and c < 2 and isinstance(p, int) and p in (0, top + 1):
            there = heard.at[t - 1, 0 if p == 0 else 1]
            return there[c], pltpu.roll(there[2], lanes // 2, 1) if c else there[2]
        return fa[c, p], fb[c, p]

    def minus(u, v):
        return u[0] - v[0], u[1] - v[1]

    def next_x(u):
        return tuple(pltpu.roll(v, wide - 1, 0) - v for v in u)

    def last_x(u):
        return tuple(v - pltpu.roll(v, 1, 0) for v in u)

    def next_y(u):
        a, b = (pltpu.roll(v, lanes - 1, 1) for v in u)
        return jnp.where(at_last, b, a) - u[0], jnp.where(at_last, a, b) - u[1]

    def last_y(u):
        a, b = (pltpu.roll(v, 1, 1) for v in u)
        return u[0] - jnp.where(at_first, b, a), u[1] - jnp.where(at_first, a, b)

    def put(c, p, value, t):
        fa[c, p], fb[c, p] = value
        if t == STEPS and not (isinstance(p, int) and not LOW <= p < top):
            out_ref[c, p - LOW] = value[0][:rows]

    def magnetic(p, t):
        low = isinstance(p, int) and p < LOW
        rate = low_rate if low else COURANT
        outer = isinstance(p, int) and p == 0

        def push(c, curl):
            old = fa[c, p], fb[c, p]
            put(c, p, tuple(o - rate * k for o, k in zip(old, curl)), t)

        ex, ey, ez = pair(0, p, t - 1), pair(1, p, t - 1), pair(2, p)
        push(3, minus(next_y(ez), minus(pair(1, p + 1, t - 1), ey)))
        push(4, minus(minus(pair(0, p + 1, t - 1), ex), next_x(ez)))
        if not outer:
            push(5, minus(next_x(ey), next_y(ex)))

    def electric(p, t):
        coef = ca[p], cb[p]

        def push(c, curl):
            old = fa[c, p], fb[c, p]
            put(c, p, tuple(o + k * d for o, k, d in zip(old, coef, curl)), t)

        hx, hy = pair(3, p), pair(4, p)
        push(2, minus(last_x(hy), last_y(hx)))
        if isinstance(p, int) and p == 0:
            return
        hz = pair(5, p)
        here = (gz * depth + p - LOW == plane_ref[0]).astype(jnp.float32)
        pushed = wave_ref[t - 1] * here
        curl = minus(last_y(hz), minus(hy, pair(4, p - 1)))
        push(0, (curl[0] + pushed * prof_a[...], curl[1] + pushed * prof_b[...]))
        push(1, minus(minus(hx, pair(3, p - 1)), last_x(hz)))

    def gather(p, t):
        total = jnp.zeros((rows, lanes), jnp.float32) if t == 1 else grad_ref[p - LOW]
        for c in range(3):
            total = total + stored[t - 1, c, p - LOW].astype(jnp.float32) * fa[c, p, own]
        if t == STEPS:
            total = jnp.where(mat[p, own] >= 2, -total, 0.0)
        grad_ref[p - LOW] = total

    def tell(t):
        copies = []
        for k, (p, by) in enumerate(((top - 2, 1), (LOW + 1, -1))):
            words = said.at[t - 1, k]
            words[0], words[1] = fa[0, p], fa[1, p]
            middle = (lane >= lanes // 4) & (lane < 3 * lanes // 4)
            words[2] = jnp.where(middle, pltpu.roll(fb[1, p], lanes // 2, 1), fb[0, p])
            copies.append(make(7 + 10 * k - 1 + t, words, heard.at[t - 1, k], gz=by))
        for copy in copies:
            copy.start()
        return copies

    a, b = LOW, top - 1
    run(a, b, lambda p: magnetic(p, 1))
    run(a + 1, b, lambda p: electric(p, 1))
    first_told = tell(1)
    loads[3].wait()
    run(a + 1, b, lambda p: gather(p, 1))

    for copy in planes + ghosts + borders:
        copy.arrived()
    coef_a(1)
    for c in range(6):
        fb[c, 1] = unpack(z_border[0], place(c, depth - 1)[1])
    coef_b(1, unpack(z_border[0], place(6, depth - 1)[1]))
    for c in range(6):
        fb[c, top] = unpack(z_border[1], place(c, 0)[1])
    each((1, b), lambda p: magnetic(p, 1))
    each((a, b), lambda p: electric(p, 1))
    run(a, b, lambda p: magnetic(p, 2))
    each((a, b), lambda p: gather(p, 1))
    run(a + 1, b, lambda p: electric(p, 2))
    second_told = tell(2)
    run(a + 1, b, lambda p: gather(p, 2))

    for copy in outer:
        copy.arrived()
    keep = (gz != last).astype(jnp.float32)
    coef_a(0)
    coef_a(top, keep)
    for c in range(5):
        fb[c, 0] = unpack(z_border[0], place(c, depth - 2)[1])
    coef_b(0, unpack(z_border[0], place(6, depth - 2)[1]))
    coef_b(top, unpack(z_border[1], place(6, 0)[1]), keep)
    for c in range(2):
        fb[c, top + 1] = unpack(z_border[1], place(c, 1)[1])
    each((0, top), lambda p: magnetic(p, 1))
    each((0, 1, top), lambda p: electric(p, 1))
    each((1, b), lambda p: magnetic(p, 2))
    each((a, b), lambda p: electric(p, 2))
    each((a, b), lambda p: gather(p, 2))
    run(a, b, lambda p: magnetic(p, 3))
    run(a + 1, b, lambda p: electric(p, 3))
    run(a + 1, b, lambda p: gather(p, 3))
    magnetic(a + 1, 4)

    for copy in first_told:
        copy.arrived()
    each((0, top), lambda p: magnetic(p, 2))
    each((0, 1, top), lambda p: electric(p, 2))
    each((1, b), lambda p: magnetic(p, 3))
    each((a, b), lambda p: electric(p, 3))
    each((a, b), lambda p: gather(p, 3))
    each((a, b - 1), lambda p: magnetic(p, 4))
    each((a + 1, b - 1), lambda p: electric(p, 4))
    each((a + 1, b - 1), lambda p: gather(p, 4))

    for copy in second_told:
        copy.arrived()
    each((0, top), lambda p: magnetic(p, 3))
    each((1, top), lambda p: electric(p, 3))
    each((1, b), lambda p: magnetic(p, 4))
    each((a, b), lambda p: electric(p, 4))
    each((a, b), lambda p: gather(p, 4))

    for copy in planes + outer + tiles + columns + ghosts + corners + borders + first_told + second_told:
        copy.sent()


def on_device(
    fields_in, material, material_eps, source_plane, source_wave, source_profile, forward_fields
):
    depth, rows, lanes = material.shape
    wide = rows + 2 * HALO
    levels = depth + 2 * LOW
    f32 = jnp.float32
    whole = pl.BlockSpec(memory_space=pltpu.VMEM)
    scalars = pl.BlockSpec(memory_space=pltpu.SMEM)
    remote = pl.BlockSpec(memory_space=pltpu.HBM)
    return pl.pallas_call(
        kernel,
        out_shape=(
            jax.ShapeDtypeStruct(fields_in.shape, f32),
            jax.ShapeDtypeStruct(material.shape, f32),
        ),
        in_specs=[scalars] * 3 + [remote] * 4,
        out_specs=(whole, whole),
        scratch_shapes=[
            pltpu.VMEM((6, levels, wide, lanes), f32),
            pltpu.VMEM((6, levels, wide, lanes), f32),
            pltpu.VMEM((levels, wide, lanes), f32),
            pltpu.VMEM((levels, wide, lanes), f32),
            pltpu.VMEM((levels, wide, lanes), jnp.int32),
            pltpu.VMEM((wide, lanes), f32),
            pltpu.VMEM((wide, lanes), f32),
            pltpu.VMEM(forward_fields.shape, forward_fields.dtype),
            pltpu.VMEM((2, rows, lanes), f32),
            pltpu.VMEM((2, 2, rows, lanes), f32),
            pltpu.VMEM((2, wide, lanes), f32),
            pltpu.VMEM((2, wide, lanes), f32),
            pltpu.VMEM((2, 6, depth // 2, 8, lanes), f32),
            pltpu.VMEM((2, depth // 2, 8, lanes), jnp.int32),
            pltpu.VMEM((2, 6, depth // 2, 8, lanes), f32),
            pltpu.VMEM((2, depth // 2, 8, lanes), jnp.int32),
            pltpu.VMEM((2, 8, lanes), f32),
            pltpu.VMEM((2, 2, 2, 8, lanes), f32),
            pltpu.VMEM((6, depth, 8, lanes), f32),
            pltpu.VMEM((depth, 8, lanes), jnp.int32),
            pltpu.VMEM((2, 2, 3, wide, lanes), f32),
            pltpu.VMEM((2, 2, 3, wide, lanes), f32),
            pltpu.SemaphoreType.DMA((4,)),
            pltpu.SemaphoreType.DMA((COPIES,)),
            pltpu.SemaphoreType.DMA((COPIES,)),
        ],
        compiler_params=pltpu.CompilerParams(
            collective_id=0, has_side_effects=True, vmem_limit_bytes=60 << 20
        ),
    )(
        material_eps,
        source_plane,
        source_wave,
        fields_in,
        material,
        source_profile,
        forward_fields,
    )


def solution(mesh):
    placed = (
        P(None, "gz", "gx", "gy"),
        P("gz", "gx", "gy"),
        P(),
        P(),
        P(),
        P("gx", "gy"),
        P(None, None, "gz", "gx", "gy"),
    )
    return jax.shard_map(
        on_device,
        mesh=mesh,
        in_specs=placed,
        out_specs=(P(None, "gz", "gx", "gy"), P("gz", "gx", "gy")),
        check_vma=False,
    )
```

```python
import functools

import jax
import jax.numpy as jnp
from jax import lax
from jax.experimental import pallas as pl
from jax.experimental.pallas import tpu as pltpu
from jax.sharding import PartitionSpec as P

COURANT = 0.5
MESH = pl.DeviceIdType.MESH
STEPS = 4
LOW = 2
HALO = 4
SLOT = 2 * HALO
COPIES = 31
CHIPS_Z = 16


def around(axis, by):
    size = lax.axis_size(axis)
    return lax.rem(lax.axis_index(axis) + by + size, size)


class Copy:
    def __init__(self, k, src, dst, send, recv, **steps):
        self.end = "gz" in steps
        by = steps.get("gz", 1)
        last = lax.axis_size("gz") - 1
        self.sends = lax.axis_index("gz") != (last if by > 0 else 0)
        self.takes = lax.axis_index("gz") != (0 if by > 0 else last)
        self.copy = pltpu.make_async_remote_copy(
            src_ref=src,
            dst_ref=dst,
            send_sem=send.at[k],
            recv_sem=recv.at[k],
            device_id={axis: around(axis, n) for axis, n in steps.items()},
            device_id_type=MESH,
        )

    def _on(self, flag, act):
        if self.end:
            pl.when(flag)(act)
        else:
            act()

    def start(self):
        self._on(self.sends, self.copy.start)

    def sent(self):
        self._on(self.sends, self.copy.wait_send)

    def arrived(self):
        self._on(self.takes, self.copy.wait_recv)


def each(planes, act):
    for p in planes:
        act(p)


def run(lo, hi, act):
    if hi - lo == 1:
        act(lo)
    else:
        lax.fori_loop(lo, hi, lambda p, _: (act(p), 0)[1], 0)


def kernel(
    eps_ref,
    plane_ref,
    wave_ref,
    fields,
    material,
    profile,
    forward,
    out,
    grad,
    out_ref,
    grad_ref,
    fa,
    fb,
    ca,
    cb,
    mat,
    prof_a,
    prof_b,
    stored,
    packed,
    y_in,
    border,
    z_border,
    x_pack,
    x_mat_pack,
    x_in,
    x_mat_in,
    x_prof_in,
    x_border_in,
    x_out,
    x_mat_out,
    said,
    heard,
    heard_b,
    local,
    send,
    recv,
):
    _, depth, rows, lanes = fields.shape
    wide = rows + 2 * HALO
    own = pl.ds(0, rows)
    extra = pl.ds(rows, 2 * HALO)
    first, final = pl.ds(0, 8), pl.ds(rows - 8, 8)
    top = LOW + depth
    gz, last = lax.axis_index("gz"), lax.axis_size("gz") - 1
    make = functools.partial(Copy, send=send, recv=recv)

    barrier = pltpu.get_barrier_semaphore()

    def greet(**steps):
        there = {axis: around(axis, n) for axis, n in steps.items()}
        pl.semaphore_signal(barrier, inc=1, device_id=there, device_id_type=MESH)

    pl.when(gz != last)(lambda: greet(gz=1))
    pl.when(gz != 0)(lambda: greet(gz=-1))
    for by in (1, -1):
        greet(gx=by)
        greet(gy=by)
        for n in (1, -1):
            greet(gx=by, gy=n)
    loads = [
        pltpu.make_async_copy(src, dst, local.at[k])
        for k, (src, dst) in enumerate(
            (
                (fields, fa.at[:, pl.ds(LOW, depth), own]),
                (material, mat.at[pl.ds(LOW, depth), own]),
                (profile, prof_a.at[own]),
                (forward, stored),
            )
        )
    ]
    for load in loads[:3]:
        load.start()
    edge = (gz == 0) | (gz == last)
    pl.semaphore_wait(barrier, jnp.where(edge, 9, 10))

    falling = [
        make(9, fields.at[:, 0], fa.at[:, top, own], gz=-1),
        make(12, material.at[0], mat.at[top, own], gz=-1),
    ]
    rising = [
        make(0, fields.at[:, depth - 1], fa.at[:, 1, own], gz=1),
        make(2, material.at[pl.ds(depth - 2, 2)], mat.at[pl.ds(0, 2), own], gz=1),
    ]
    outer = [
        make(1, fields.at[pl.ds(0, 5), depth - 2], fa.at[pl.ds(0, 5), 0, own], gz=1),
        make(11, fields.at[pl.ds(0, 2), 1], fa.at[pl.ds(0, 2), top + 1, own], gz=-1),
    ]
    planes = falling + rising
    turn = gz % CHIPS_Z == 0
    for copy in rising:
        copy.start()

    @pl.when(~turn)
    def _():
        for copy in falling:
            copy.start()

    lane = lax.broadcasted_iota(jnp.int32, (wide, lanes), 1)
    tile_row = lax.broadcasted_iota(jnp.int32, (8, lanes), 0)
    from_next = tile_row < HALO
    at_first, at_last = lane == 0, lane == lanes - 1

    for load in loads[:3]:
        load.wait()

    def turned(tile):
        return pltpu.roll(tile, HALO, 0)

    tiles = []
    for k, (by, edge) in enumerate(((-1, first), (1, final))):
        for h in range(depth // 2):
            p = LOW + 2 * h
            for source, dest in [(fa.at[c], x_pack.at[k, c, h]) for c in range(6)] + [
                (mat, x_mat_pack.at[k, h])
            ]:
                one, two = source[p, edge], source[p + 1, edge]
                one, two = (one, turned(two)) if k == 0 else (turned(one), two)
                dest[...] = jnp.where(from_next, one, two)
        tiles += [
            make(19 + 3 * k, x_pack.at[k], x_in.at[k], gx=by),
            make(20 + 3 * k, x_mat_pack.at[k], x_mat_in.at[k], gx=by),
            make(21 + 3 * k, profile.at[edge], x_prof_in.at[k], gx=by),
        ]
    for copy in tiles:
        copy.start()

    def narrow(c, p):
        return mat[LOW + p, own].astype(jnp.float32) if c == 6 else fa[c, LOW + p, own]

    def place(c, p):
        return p // 2, 7 * (p % 2) + c

    profile_place = (0, 14)
    slot_of = lane[:rows] // SLOT
    for half in range(2):
        filled = jnp.zeros((rows, lanes), jnp.float32)
        pieces = [(place(c, p)[1], narrow(c, p)) for p in (2 * half, 2 * half + 1) for c in range(7)]
        if half == profile_place[0]:
            pieces.append((profile_place[1], prof_a[own]))
        for s, value in pieces:
            filled = jnp.where(slot_of == s, pltpu.roll(value, SLOT * s + HALO, 1), filled)
        packed[half] = filled
    columns = [make(29 + k, packed, y_in.at[k], gy=by) for k, by in enumerate((-1, 1))]
    corners = [
        make(25 + 2 * k + n, packed.at[:, edge], x_border_in.at[k, n], gx=by, gy=way)
        for k, (by, edge) in enumerate(((-1, first), (1, final)))
        for n, way in enumerate((-1, 1))
    ]
    for copy in corners + columns:
        copy.start()
    loads[3].start()

    @pl.when(gz == 0)
    def _():
        fa[:, pl.ds(0, LOW)] = jnp.zeros((6, LOW, wide, lanes), jnp.float32)
        mat[pl.ds(0, LOW)] = jnp.zeros((LOW, wide, lanes), jnp.int32)
        z_border[0] = jnp.zeros(z_border.shape[1:], jnp.float32)
        for m in range(2):
            heard[m, 0] = jnp.zeros(heard.shape[2:], jnp.float32)

    @pl.when(gz == last)
    def _():
        fa[:, pl.ds(top, 2)] = jnp.zeros((6, 2, wide, lanes), jnp.float32)
        mat[top] = jnp.zeros((wide, lanes), jnp.int32)
        z_border[1] = jnp.zeros(z_border.shape[1:], jnp.float32)
        for m in range(2):
            heard[m, 1] = jnp.zeros(heard.shape[2:], jnp.float32)

    for copy in tiles:
        copy.arrived()

    @pl.when(turn)
    def _():
        for copy in falling:
            copy.start()

    def meet(after, before, p):
        after, before = (turned(after), before) if p % 2 else (after, turned(before))
        return jnp.where(from_next, after, before)

    for c in range(6):
        for p in range(depth):
            tile = meet(x_in[0, c, p // 2], x_in[1, c, p // 2], p)
            x_out[c, p] = tile
            fa[c, LOW + p, extra] = tile
    for p in range(depth):
        tile = meet(x_mat_in[0, p // 2], x_mat_in[1, p // 2], p)
        x_mat_out[p] = tile
        mat[LOW + p, extra] = tile
    prof_a[extra] = jnp.where(from_next, x_prof_in[0], x_prof_in[1])
    ghosts = [
        make(13, x_out.at[:, 0], fa.at[:, top, extra], gz=-1),
        make(15, x_mat_out.at[0], mat.at[top, extra], gz=-1),
        make(3, x_out.at[:, depth - 1], fa.at[:, 1, extra], gz=1),
        make(5, x_mat_out.at[pl.ds(depth - 2, 2)], mat.at[pl.ds(0, 2), extra], gz=1),
    ]
    outer += [
        make(4, x_out.at[pl.ds(0, 5), depth - 2], fa.at[pl.ds(0, 5), 0, extra], gz=1),
        make(14, x_out.at[pl.ds(0, 2), 1], fa.at[pl.ds(0, 2), top + 1, extra], gz=-1),
    ]
    for copy in ghosts:
        copy.start()

    for copy in columns:
        copy.arrived()
    from_below = lane % SLOT < HALO
    for half in range(2):
        border[half, own] = jnp.where(from_below[:rows], y_in[1, half], y_in[0, half])
    table = [COURANT / jnp.full((1, lanes), eps_ref[m], jnp.float32) for m in range(eps_ref.shape[0])]

    def coef_a(p, keep=None):
        kinds = mat[p]
        value = jnp.broadcast_to(table[0], (wide, lanes))
        for m in range(1, len(table)):
            value = jnp.where(kinds == m, table[m], value)
        ca[p] = value if keep is None else value * keep

    def coef_b(p, kinds, keep=None):
        value = jnp.broadcast_to(table[0], kinds.shape)
        for m in range(1, len(table)):
            value = jnp.where(kinds > m - 0.5, table[m], value)
        cb[p] = value if keep is None else value * keep

    def unpack(value, s):
        return pltpu.roll(value, lanes - (SLOT * s + HALO), 1)

    run(LOW, top, coef_a)
    for copy in corners:
        copy.arrived()
    for half in range(2):
        tile = jnp.where(from_next, x_border_in[0, :, half], x_border_in[1, :, half])
        border[half, extra] = jnp.where(from_below[:8], tile[1], tile[0])
    borders = [
        make(6, border.at[1], z_border.at[0], gz=1),
        make(16, border.at[0], z_border.at[1], gz=-1),
    ]
    for copy in borders + outer:
        copy.start()

    for p in range(depth):
        for c in range(6):
            fb[c, LOW + p] = unpack(border[place(c, p)[0]], place(c, p)[1])
        coef_b(LOW + p, unpack(border[place(6, p)[0]], place(6, p)[1]))
    prof_b[...] = unpack(border[profile_place[0]], profile_place[1])

    low_rate = COURANT * (gz != 0).astype(jnp.float32)

    def pair(c, p, t=0):
        if t > 0 and c < 2 and isinstance(p, int) and p in (0, top + 1):
            side = 0 if p == 0 else 1
            return heard[t - 1, side, pl.ds(c * wide, wide)], heard_b[t - 1, side, c]
        return fa[c, p], fb[c, p]

    def minus(u, v):
        return u[0] - v[0], u[1] - v[1]

    def next_x(u):
        return tuple(pltpu.roll(v, wide - 1, 0) - v for v in u)

    def last_x(u):
        return tuple(v - pltpu.roll(v, 1, 0) for v in u)

    def next_y(u):
        a, b = (pltpu.roll(v, lanes - 1, 1) for v in u)
        return jnp.where(at_last, b, a) - u[0], jnp.where(at_last, a, b) - u[1]

    def last_y(u):
        a, b = (pltpu.roll(v, 1, 1) for v in u)
        return u[0] - jnp.where(at_first, b, a), u[1] - jnp.where(at_first, a, b)

    def put(c, p, value, t):
        fa[c, p] = value[0]
        if t < STEPS or c > 2:
            fb[c, p] = value[1]
        if t == STEPS and not (isinstance(p, int) and not LOW <= p < top):
            out_ref[c, p - LOW] = value[0][:rows]

    def magnetic(p, t):
        low = isinstance(p, int) and p < LOW
        rate = low_rate if low else COURANT
        outer = isinstance(p, int) and (p == 0 or p < LOW and t == STEPS)

        def push(c, curl):
            old = fa[c, p], fb[c, p]
            put(c, p, tuple(o - rate * k for o, k in zip(old, curl)), t)

        ex, ey, ez = pair(0, p, t - 1), pair(1, p, t - 1), pair(2, p)
        push(3, minus(next_y(ez), minus(pair(1, p + 1, t - 1), ey)))
        push(4, minus(minus(pair(0, p + 1, t - 1), ex), next_x(ez)))
        if not outer:
            push(5, minus(next_x(ey), next_y(ex)))

    def electric(p, t):
        coef = ca[p], cb[p]

        def push(c, curl):
            old = fa[c, p], fb[c, p]
            put(c, p, tuple(o + k * d for o, k, d in zip(old, coef, curl)), t)

        hx, hy = pair(3, p), pair(4, p)
        if not (isinstance(p, int) and p == top and t == STEPS - 1):
            push(2, minus(last_x(hy), last_y(hx)))
        if isinstance(p, int) and p == 0:
            return
        hz = pair(5, p)
        here = (gz * depth + p - LOW == plane_ref[0]).astype(jnp.float32)
        pushed = wave_ref[t - 1] * here
        curl = minus(last_y(hz), minus(hy, pair(4, p - 1)))
        push(0, (curl[0] + pushed * prof_a[...], curl[1] + pushed * prof_b[...]))
        push(1, minus(minus(hx, pair(3, p - 1)), last_x(hz)))

    def gather(p, t):
        total = jnp.zeros((rows, lanes), jnp.float32) if t == 1 else grad_ref[p - LOW]
        for c in range(3):
            total = total + stored[t - 1, c, p - LOW].astype(jnp.float32) * fa[c, p, own]
        if t == STEPS:
            total = jnp.where(mat[p, own] >= 2, -total, 0.0)
        grad_ref[p - LOW] = total

    folds = lanes // (2 * SLOT)
    fold = ((lane[:8] + HALO) % lanes) // (2 * SLOT)

    def unfold(t):
        for side in range(2):
            for i in range(folds + 1):
                part = heard[t - 1, side, pl.ds(2 * wide + 8 * (i // folds), 8)]
                for c in range(2):
                    by = (2 * SLOT * (i % folds) + SLOT * c) % lanes
                    heard_b[t - 1, side, c, pl.ds(8 * i, 8)] = (
                        pltpu.roll(part, lanes - by, 1) if by else part
                    )

    def tell(t):
        copies = []
        for k, (p, by) in enumerate(((top - 2, 1), (LOW + 1, -1))):
            words = said.at[t - 1, k]
            words[pl.ds(0, wide)], words[pl.ds(wide, wide)] = fa[0, p], fa[1, p]
            ghost = jnp.where(
                (lane >= HALO) & (lane < HALO + SLOT), pltpu.roll(fb[1, p], SLOT, 1), fb[0, p]
            )
            filled = ghost[:8]
            for i in range(1, folds):
                turn_by = 2 * SLOT * i
                part = pltpu.roll(ghost[8 * i : 8 * i + 8], turn_by, 1)
                filled = jnp.where(fold == i, part, filled)
            words[pl.ds(2 * wide, 8)] = filled
            words[pl.ds(2 * wide + 8, 8)] = ghost[8 * folds :]
            copies.append(make(7 + 10 * k - 1 + t, words, heard.at[t - 1, k], gz=by))
        for copy in copies:
            copy.start()
        return copies

    a, b = LOW, top - 1
    run(a, b, lambda p: magnetic(p, 1))
    run(a + 1, b, lambda p: electric(p, 1))
    first_told = tell(1)
    loads[3].wait()
    run(a + 1, b, lambda p: gather(p, 1))

    for copy in planes + ghosts + borders:
        copy.arrived()
    coef_a(1)
    for c in range(6):
        fb[c, 1] = unpack(z_border[0], place(c, depth - 1)[1])
    coef_b(1, unpack(z_border[0], place(6, depth - 1)[1]))
    for c in range(6):
        fb[c, top] = unpack(z_border[1], place(c, 0)[1])
    each((1, b), lambda p: magnetic(p, 1))
    each((a, b), lambda p: electric(p, 1))
    run(a, b, lambda p: magnetic(p, 2))
    run(a + 1, b, lambda p: electric(p, 2))
    second_told = tell(2)
    each((a, b), lambda p: gather(p, 1))
    run(a + 1, b, lambda p: gather(p, 2))

    for copy in outer:
        copy.arrived()
    keep = (gz != last).astype(jnp.float32)
    coef_a(0)
    coef_a(top, keep)
    for c in range(5):
        fb[c, 0] = unpack(z_border[0], place(c, depth - 2)[1])
    coef_b(0, unpack(z_border[0], place(6, depth - 2)[1]))
    coef_b(top, unpack(z_border[1], place(6, 0)[1]), keep)
    for c in range(2):
        fb[c, top + 1] = unpack(z_border[1], place(c, 1)[1])
    each((0, top), lambda p: magnetic(p, 1))
    each((0, 1, top), lambda p: electric(p, 1))
    each((1, b), lambda p: magnetic(p, 2))
    each((a, b), lambda p: electric(p, 2))
    each((a, b), lambda p: gather(p, 2))
    run(a, b, lambda p: magnetic(p, 3))
    run(a + 1, b, lambda p: electric(p, 3))
    run(a + 1, b, lambda p: gather(p, 3))
    magnetic(a + 1, 4)

    for copy in first_told:
        copy.arrived()
    unfold(1)
    each((0, top), lambda p: magnetic(p, 2))
    each((0, 1, top), lambda p: electric(p, 2))
    each((1, b), lambda p: magnetic(p, 3))
    each((a, b), lambda p: electric(p, 3))
    each((a, b), lambda p: gather(p, 3))
    each((a, b - 1), lambda p: magnetic(p, 4))
    each((a + 1, b - 1), lambda p: electric(p, 4))
    each((a + 1, b - 1), lambda p: gather(p, 4))

    stores = []

    def store(planes_at):
        for k, (src, dst) in enumerate(((out_ref, out), (grad_ref, grad))):
            there = (slice(None), planes_at) if k == 0 else (planes_at,)
            stores.append(
                pltpu.make_async_copy(src.at[there], dst.at[there], local.at[4 + len(stores)])
            )
            stores[-1].start()

    store(pl.ds(1, depth - 2))
    for copy in second_told:
        copy.arrived()
    unfold(2)
    each((0, top), lambda p: magnetic(p, 3))
    each((1, top), lambda p: electric(p, 3))
    each((1, b), lambda p: magnetic(p, 4))
    each((a, b), lambda p: electric(p, 4))
    each((a, b), lambda p: gather(p, 4))

    store(pl.ds(0, 1))
    store(pl.ds(depth - 1, 1))
    for copy in stores:
        copy.wait()
    for copy in planes + outer + tiles + columns + ghosts + corners + borders + first_told + second_told:
        copy.sent()


def hand_on(fields, grad, fields_out, grad_out, staged, staged_grad, sem):
    parts = [(fields.at[c], staged.at[c], fields_out.at[c]) for c in range(6)]
    parts.append((grad, staged_grad, grad_out))
    inward = [pltpu.make_async_copy(a, b, sem.at[k]) for k, (a, b, _) in enumerate(parts)]
    outward = [pltpu.make_async_copy(b, c, sem.at[7 + k]) for k, (_, b, c) in enumerate(parts)]
    for copy in inward:
        copy.start()
    for one, two in zip(inward, outward):
        one.wait()
        two.start()
    for copy in outward:
        copy.wait()


def on_device(
    fields_in, material, material_eps, source_plane, source_wave, source_profile, forward_fields
):
    depth, rows, lanes = material.shape
    wide = rows + 2 * HALO
    levels = depth + 2 * LOW
    f32 = jnp.float32
    scalars = pl.BlockSpec(memory_space=pltpu.SMEM)
    remote = pl.BlockSpec(memory_space=pltpu.HBM)
    fields_out, eps_grad = pl.pallas_call(
        kernel,
        out_shape=(
            jax.ShapeDtypeStruct(fields_in.shape, f32),
            jax.ShapeDtypeStruct(material.shape, f32),
        ),
        in_specs=[scalars] * 3 + [remote] * 4,
        out_specs=(remote, remote),
        scratch_shapes=[
            pltpu.VMEM(fields_in.shape, f32),
            pltpu.VMEM(material.shape, f32),
            pltpu.VMEM((6, levels, wide, lanes), f32),
            pltpu.VMEM((6, levels, wide, lanes), f32),
            pltpu.VMEM((levels, wide, lanes), f32),
            pltpu.VMEM((levels, wide, lanes), f32),
            pltpu.VMEM((levels, wide, lanes), jnp.int32),
            pltpu.VMEM((wide, lanes), f32),
            pltpu.VMEM((wide, lanes), f32),
            pltpu.VMEM(forward_fields.shape, forward_fields.dtype),
            pltpu.VMEM((2, rows, lanes), f32),
            pltpu.VMEM((2, 2, rows, lanes), f32),
            pltpu.VMEM((2, wide, lanes), f32),
            pltpu.VMEM((2, wide, lanes), f32),
            pltpu.VMEM((2, 6, depth // 2, 8, lanes), f32),
            pltpu.VMEM((2, depth // 2, 8, lanes), jnp.int32),
            pltpu.VMEM((2, 6, depth // 2, 8, lanes), f32),
            pltpu.VMEM((2, depth // 2, 8, lanes), jnp.int32),
            pltpu.VMEM((2, 8, lanes), f32),
            pltpu.VMEM((2, 2, 2, 8, lanes), f32),
            pltpu.VMEM((6, depth, 8, lanes), f32),
            pltpu.VMEM((depth, 8, lanes), jnp.int32),
            pltpu.VMEM((2, 2, 2 * wide + 16, lanes), f32),
            pltpu.VMEM((2, 2, 2 * wide + 16, lanes), f32),
            pltpu.VMEM((2, 2, 2, wide, lanes), f32),
            pltpu.SemaphoreType.DMA((10,)),
            pltpu.SemaphoreType.DMA((COPIES,)),
            pltpu.SemaphoreType.DMA((COPIES,)),
        ],
        compiler_params=pltpu.CompilerParams(
            collective_id=0, has_side_effects=True, vmem_limit_bytes=60 << 20
        ),
    )(
        material_eps,
        source_plane,
        source_wave,
        fields_in,
        material,
        source_profile,
        forward_fields,
    )
    return pl.pallas_call(
        hand_on,
        out_shape=(
            jax.ShapeDtypeStruct(fields_in.shape, f32),
            jax.ShapeDtypeStruct(material.shape, f32),
        ),
        in_specs=[remote] * 2,
        out_specs=(remote, remote),
        scratch_shapes=[
            pltpu.VMEM(fields_in.shape, f32),
            pltpu.VMEM(material.shape, f32),
            pltpu.SemaphoreType.DMA((14,)),
        ],
        compiler_params=pltpu.CompilerParams(vmem_limit_bytes=60 << 20),
    )(fields_out, eps_grad)


def solution(mesh):
    placed = (
        P(None, "gz", "gx", "gy"),
        P("gz", "gx", "gy"),
        P(),
        P(),
        P(),
        P("gx", "gy"),
        P(None, None, "gz", "gx", "gy"),
    )
    return jax.shard_map(
        on_device,
        mesh=mesh,
        in_specs=placed,
        out_specs=(P(None, "gz", "gx", "gy"), P("gz", "gx", "gy")),
        check_vma=False,
    )
```

```python
import functools

import jax
import jax.numpy as jnp
from jax import lax
from jax.experimental import pallas as pl
from jax.experimental.pallas import tpu as pltpu
from jax.sharding import PartitionSpec as P

COURANT = 0.5
MESH = pl.DeviceIdType.MESH
STEPS = 4
LOW = 2
HALO = 4
SLOT = 2 * HALO
COPIES = 31
CHIPS_Z = 16


def around(axis, by):
    size = lax.axis_size(axis)
    return lax.rem(lax.axis_index(axis) + by + size, size)


class Copy:
    def __init__(self, k, src, dst, send, recv, **steps):
        self.end = "gz" in steps
        by = steps.get("gz", 1)
        last = lax.axis_size("gz") - 1
        self.sends = lax.axis_index("gz") != (last if by > 0 else 0)
        self.takes = lax.axis_index("gz") != (0 if by > 0 else last)
        self.copy = pltpu.make_async_remote_copy(
            src_ref=src,
            dst_ref=dst,
            send_sem=send.at[k],
            recv_sem=recv.at[k],
            device_id={axis: around(axis, n) for axis, n in steps.items()},
            device_id_type=MESH,
        )

    def _on(self, flag, act):
        if self.end:
            pl.when(flag)(act)
        else:
            act()

    def start(self):
        self._on(self.sends, self.copy.start)

    def sent(self):
        self._on(self.sends, self.copy.wait_send)

    def arrived(self):
        self._on(self.takes, self.copy.wait_recv)


def each(planes, act):
    for p in planes:
        act(p)


def run(lo, hi, act):
    if hi - lo == 1:
        act(lo)
    else:
        lax.fori_loop(lo, hi, lambda p, _: (act(p), 0)[1], 0)


def kernel(
    eps_ref,
    plane_ref,
    wave_ref,
    fields,
    material,
    profile,
    forward,
    out,
    grad,
    out_ref,
    grad_ref,
    fa,
    fb,
    ca,
    cb,
    mat,
    prof_a,
    prof_b,
    stored,
    packed,
    y_in,
    border,
    z_border,
    x_pack,
    x_mat_pack,
    near,
    x_in,
    x_mat_in,
    x_prof_in,
    x_border_in,
    x_out,
    x_mat_out,
    said,
    heard,
    heard_b,
    local,
    send,
    recv,
):
    _, depth, rows, lanes = fields.shape
    wide = rows + 2 * HALO
    own = pl.ds(0, rows)
    extra = pl.ds(rows, 2 * HALO)
    first, final = pl.ds(0, 8), pl.ds(rows - 8, 8)
    top = LOW + depth
    gz, last = lax.axis_index("gz"), lax.axis_size("gz") - 1
    make = functools.partial(Copy, send=send, recv=recv)

    barrier = pltpu.get_barrier_semaphore()

    def greet(**steps):
        there = {axis: around(axis, n) for axis, n in steps.items()}
        pl.semaphore_signal(barrier, inc=1, device_id=there, device_id_type=MESH)

    pl.when(gz != last)(lambda: greet(gz=1))
    pl.when(gz != 0)(lambda: greet(gz=-1))
    for by in (1, -1):
        greet(gx=by)
        greet(gy=by)
        for n in (1, -1):
            greet(gx=by, gy=n)
    loads = [
        pltpu.make_async_copy(src, dst, local.at[k])
        for k, (src, dst) in enumerate(
            (
                (fields, fa.at[:, pl.ds(LOW, depth), own]),
                (material, mat.at[pl.ds(LOW, depth), own]),
                (profile, prof_a.at[own]),
                (forward, stored),
            )
        )
    ]
    edges = [
        pltpu.make_async_copy(fields.at[:, :, edge], near.at[k], local.at[10 + k])
        for k, edge in enumerate((first, final))
    ]
    for load in edges + [loads[1], loads[0], loads[2]]:
        load.start()
    edge = (gz == 0) | (gz == last)
    pl.semaphore_wait(barrier, jnp.where(edge, 9, 10))

    falling = [
        make(9, fields.at[:, 0], fa.at[:, top, own], gz=-1),
        make(12, material.at[0], mat.at[top, own], gz=-1),
    ]
    rising = [
        make(0, fields.at[:, depth - 1], fa.at[:, 1, own], gz=1),
        make(2, material.at[pl.ds(depth - 2, 2)], mat.at[pl.ds(0, 2), own], gz=1),
    ]
    outer = [
        make(1, fields.at[pl.ds(0, 5), depth - 2], fa.at[pl.ds(0, 5), 0, own], gz=1),
        make(11, fields.at[pl.ds(0, 2), 1], fa.at[pl.ds(0, 2), top + 1, own], gz=-1),
    ]
    planes = falling + rising
    turn = gz % CHIPS_Z == 0
    for copy in rising:
        copy.start()

    @pl.when(~turn)
    def _():
        for copy in falling:
            copy.start()

    lane = lax.broadcasted_iota(jnp.int32, (wide, lanes), 1)
    tile_row = lax.broadcasted_iota(jnp.int32, (8, lanes), 0)
    from_next = tile_row < HALO
    at_first, at_last = lane == 0, lane == lanes - 1

    for load in edges + [loads[1]]:
        load.wait()

    def turned(tile):
        return pltpu.roll(tile, HALO, 0)

    tiles = []
    for k, (by, edge) in enumerate(((-1, first), (1, final))):
        for h in range(depth // 2):
            p = LOW + 2 * h
            pairs = [(near[k, c, 2 * h], near[k, c, 2 * h + 1], x_pack.at[k, c, h]) for c in range(6)]
            for one, two, dest in pairs + [(mat[p, edge], mat[p + 1, edge], x_mat_pack.at[k, h])]:
                one, two = (one, turned(two)) if k == 0 else (turned(one), two)
                dest[...] = jnp.where(from_next, one, two)
        tiles += [
            make(19 + 3 * k, x_pack.at[k], x_in.at[k], gx=by),
            make(20 + 3 * k, x_mat_pack.at[k], x_mat_in.at[k], gx=by),
            make(21 + 3 * k, profile.at[edge], x_prof_in.at[k], gx=by),
        ]
    for copy in tiles:
        copy.start()
    loads[0].wait()
    loads[2].wait()

    def narrow(c, p):
        return mat[LOW + p, own].astype(jnp.float32) if c == 6 else fa[c, LOW + p, own]

    def place(c, p):
        return p // 2, 7 * (p % 2) + c

    profile_place = (0, 14)
    slot_of = lane[:rows] // SLOT
    for half in range(2):
        filled = jnp.zeros((rows, lanes), jnp.float32)
        pieces = [(place(c, p)[1], narrow(c, p)) for p in (2 * half, 2 * half + 1) for c in range(7)]
        if half == profile_place[0]:
            pieces.append((profile_place[1], prof_a[own]))
        for s, value in pieces:
            filled = jnp.where(slot_of == s, pltpu.roll(value, SLOT * s + HALO, 1), filled)
        packed[half] = filled
    columns = [make(29 + k, packed, y_in.at[k], gy=by) for k, by in enumerate((-1, 1))]
    corners = [
        make(25 + 2 * k + n, packed.at[:, edge], x_border_in.at[k, n], gx=by, gy=way)
        for k, (by, edge) in enumerate(((-1, first), (1, final)))
        for n, way in enumerate((-1, 1))
    ]
    for copy in corners + columns:
        copy.start()
    loads[3].start()

    @pl.when(gz == 0)
    def _():
        fa[:, pl.ds(0, LOW)] = jnp.zeros((6, LOW, wide, lanes), jnp.float32)
        mat[pl.ds(0, LOW)] = jnp.zeros((LOW, wide, lanes), jnp.int32)
        z_border[0] = jnp.zeros(z_border.shape[1:], jnp.float32)
        for m in range(2):
            heard[m, 0] = jnp.zeros(heard.shape[2:], jnp.float32)

    @pl.when(gz == last)
    def _():
        fa[:, pl.ds(top, 2)] = jnp.zeros((6, 2, wide, lanes), jnp.float32)
        mat[top] = jnp.zeros((wide, lanes), jnp.int32)
        z_border[1] = jnp.zeros(z_border.shape[1:], jnp.float32)
        for m in range(2):
            heard[m, 1] = jnp.zeros(heard.shape[2:], jnp.float32)

    for copy in tiles:
        copy.arrived()

    @pl.when(turn)
    def _():
        for copy in falling:
            copy.start()

    def meet(after, before, p):
        after, before = (turned(after), before) if p % 2 else (after, turned(before))
        return jnp.where(from_next, after, before)

    for c in range(6):
        for p in range(depth):
            tile = meet(x_in[0, c, p // 2], x_in[1, c, p // 2], p)
            x_out[c, p] = tile
            fa[c, LOW + p, extra] = tile
    for p in range(depth):
        tile = meet(x_mat_in[0, p // 2], x_mat_in[1, p // 2], p)
        x_mat_out[p] = tile
        mat[LOW + p, extra] = tile
    prof_a[extra] = jnp.where(from_next, x_prof_in[0], x_prof_in[1])
    ghosts = [
        make(13, x_out.at[:, 0], fa.at[:, top, extra], gz=-1),
        make(15, x_mat_out.at[0], mat.at[top, extra], gz=-1),
        make(3, x_out.at[:, depth - 1], fa.at[:, 1, extra], gz=1),
        make(5, x_mat_out.at[pl.ds(depth - 2, 2)], mat.at[pl.ds(0, 2), extra], gz=1),
    ]
    outer += [
        make(4, x_out.at[pl.ds(0, 5), depth - 2], fa.at[pl.ds(0, 5), 0, extra], gz=1),
        make(14, x_out.at[pl.ds(0, 2), 1], fa.at[pl.ds(0, 2), top + 1, extra], gz=-1),
    ]
    for copy in ghosts:
        copy.start()

    for copy in columns:
        copy.arrived()
    from_below = lane % SLOT < HALO
    for half in range(2):
        border[half, own] = jnp.where(from_below[:rows], y_in[1, half], y_in[0, half])
    table = [COURANT / jnp.full((1, lanes), eps_ref[m], jnp.float32) for m in range(eps_ref.shape[0])]

    def coef_a(p, keep=None):
        kinds = mat[p]
        value = jnp.broadcast_to(table[0], (wide, lanes))
        for m in range(1, len(table)):
            value = jnp.where(kinds == m, table[m], value)
        ca[p] = value if keep is None else value * keep

    def coef_b(p, kinds, keep=None):
        value = jnp.broadcast_to(table[0], kinds.shape)
        for m in range(1, len(table)):
            value = jnp.where(kinds > m - 0.5, table[m], value)
        cb[p] = value if keep is None else value * keep

    def unpack(value, s):
        return pltpu.roll(value, lanes - (SLOT * s + HALO), 1)

    run(LOW, top, coef_a)
    for copy in corners:
        copy.arrived()
    for half in range(2):
        tile = jnp.where(from_next, x_border_in[0, :, half], x_border_in[1, :, half])
        border[half, extra] = jnp.where(from_below[:8], tile[1], tile[0])
    borders = [
        make(6, border.at[1], z_border.at[0], gz=1),
        make(16, border.at[0], z_border.at[1], gz=-1),
    ]
    for copy in borders + outer:
        copy.start()

    for p in range(depth):
        for c in range(6):
            fb[c, LOW + p] = unpack(border[place(c, p)[0]], place(c, p)[1])
        coef_b(LOW + p, unpack(border[place(6, p)[0]], place(6, p)[1]))
    prof_b[...] = unpack(border[profile_place[0]], profile_place[1])

    low_rate = COURANT * (gz != 0).astype(jnp.float32)

    def pair(c, p, t=0):
        if t > 0 and c < 2 and isinstance(p, int) and p in (0, top + 1):
            side = 0 if p == 0 else 1
            return heard[t - 1, side, pl.ds(c * wide, wide)], heard_b[t - 1, side, c]
        return fa[c, p], fb[c, p]

    def minus(u, v):
        return u[0] - v[0], u[1] - v[1]

    def next_x(u):
        return tuple(pltpu.roll(v, wide - 1, 0) - v for v in u)

    def last_x(u):
        return tuple(v - pltpu.roll(v, 1, 0) for v in u)

    def next_y(u):
        a, b = (pltpu.roll(v, lanes - 1, 1) for v in u)
        return jnp.where(at_last, b, a) - u[0], jnp.where(at_last, a, b) - u[1]

    def last_y(u):
        a, b = (pltpu.roll(v, 1, 1) for v in u)
        return u[0] - jnp.where(at_first, b, a), u[1] - jnp.where(at_first, a, b)

    def put(c, p, value, t):
        fa[c, p] = value[0]
        if t < STEPS or c > 2:
            fb[c, p] = value[1]
        if t == STEPS and not (isinstance(p, int) and not LOW <= p < top):
            out_ref[c, p - LOW] = value[0][:rows]

    def magnetic(p, t):
        low = isinstance(p, int) and p < LOW
        rate = low_rate if low else COURANT
        outer = isinstance(p, int) and (p == 0 or p < LOW and t == STEPS)

        def push(c, curl):
            old = fa[c, p], fb[c, p]
            put(c, p, tuple(o - rate * k for o, k in zip(old, curl)), t)

        ex, ey, ez = pair(0, p, t - 1), pair(1, p, t - 1), pair(2, p)
        push(3, minus(next_y(ez), minus(pair(1, p + 1, t - 1), ey)))
        push(4, minus(minus(pair(0, p + 1, t - 1), ex), next_x(ez)))
        if not outer:
            push(5, minus(next_x(ey), next_y(ex)))

    def electric(p, t):
        coef = ca[p], cb[p]

        def push(c, curl):
            old = fa[c, p], fb[c, p]
            put(c, p, tuple(o + k * d for o, k, d in zip(old, coef, curl)), t)

        hx, hy = pair(3, p), pair(4, p)
        if not (isinstance(p, int) and p == top and t == STEPS - 1):
            push(2, minus(last_x(hy), last_y(hx)))
        if isinstance(p, int) and p == 0:
            return
        hz = pair(5, p)
        here = (gz * depth + p - LOW == plane_ref[0]).astype(jnp.float32)
        pushed = wave_ref[t - 1] * here
        curl = minus(last_y(hz), minus(hy, pair(4, p - 1)))
        push(0, (curl[0] + pushed * prof_a[...], curl[1] + pushed * prof_b[...]))
        push(1, minus(minus(hx, pair(3, p - 1)), last_x(hz)))

    def gather(p, t):
        total = jnp.zeros((rows, lanes), jnp.float32) if t == 1 else grad_ref[p - LOW]
        for c in range(3):
            total = total + stored[t - 1, c, p - LOW].astype(jnp.float32) * fa[c, p, own]
        if t == STEPS:
            total = jnp.where(mat[p, own] >= 2, -total, 0.0)
        grad_ref[p - LOW] = total

    folds = lanes // (2 * SLOT)
    fold = ((lane[:8] + HALO) % lanes) // (2 * SLOT)

    def unfold(t, sides=(0, 1)):
        for side in sides:
            for i in range(folds + 1):
                part = heard[t - 1, side, pl.ds(2 * wide + 8 * (i // folds), 8)]
                for c in range(2):
                    by = (2 * SLOT * (i % folds) + SLOT * c) % lanes
                    heard_b[t - 1, side, c, pl.ds(8 * i, 8)] = (
                        pltpu.roll(part, lanes - by, 1) if by else part
                    )

    def tell(t, sides=(0, 1)):
        copies = []
        for k in sides:
            p, by = ((top - 2, 1), (LOW + 1, -1))[k]
            words = said.at[t - 1, k]
            words[pl.ds(0, wide)], words[pl.ds(wide, wide)] = fa[0, p], fa[1, p]
            ghost = jnp.where(
                (lane >= HALO) & (lane < HALO + SLOT), pltpu.roll(fb[1, p], SLOT, 1), fb[0, p]
            )
            filled = ghost[:8]
            for i in range(1, folds):
                turn_by = 2 * SLOT * i
                part = pltpu.roll(ghost[8 * i : 8 * i + 8], turn_by, 1)
                filled = jnp.where(fold == i, part, filled)
            words[pl.ds(2 * wide, 8)] = filled
            words[pl.ds(2 * wide + 8, 8)] = ghost[8 * folds :]
            copies.append(make(7 + 10 * k - 1 + t, words, heard.at[t - 1, k], gz=by))
        for copy in copies:
            copy.start()
        return copies

    a, b = LOW, top - 1
    run(a, b, lambda p: magnetic(p, 1))
    run(a + 1, b, lambda p: electric(p, 1))
    first_told = tell(1)
    loads[3].wait()
    run(a + 1, b, lambda p: gather(p, 1))

    magnetic(a + 1, 2)

    for copy in falling + ghosts[:2] + borders[1:]:
        copy.arrived()
    for c in range(6):
        fb[c, top] = unpack(z_border[1], place(c, 0)[1])
    magnetic(b, 1)
    electric(b, 1)
    magnetic(b - 1, 2)
    electric(b - 1, 2)
    told_up = tell(2, (0,))

    for copy in rising + ghosts[2:] + borders[:1]:
        copy.arrived()
    coef_a(1)
    for c in range(6):
        fb[c, 1] = unpack(z_border[0], place(c, depth - 1)[1])
    coef_b(1, unpack(z_border[0], place(6, depth - 1)[1]))
    magnetic(1, 1)
    electric(a, 1)
    magnetic(a, 2)
    electric(a + 1, 2)
    told_down = tell(2, (1,))
    each((a, b), lambda p: gather(p, 1))
    run(a + 1, b, lambda p: gather(p, 2))

    for copy in outer:
        copy.arrived()
    keep = (gz != last).astype(jnp.float32)
    coef_a(0)
    coef_a(top, keep)
    for c in range(5):
        fb[c, 0] = unpack(z_border[0], place(c, depth - 2)[1])
    coef_b(0, unpack(z_border[0], place(6, depth - 2)[1]))
    coef_b(top, unpack(z_border[1], place(6, 0)[1]), keep)
    for c in range(2):
        fb[c, top + 1] = unpack(z_border[1], place(c, 1)[1])
    each((0, top), lambda p: magnetic(p, 1))
    each((0, 1, top), lambda p: electric(p, 1))
    each((1, b), lambda p: magnetic(p, 2))
    each((a, b), lambda p: electric(p, 2))
    each((a, b), lambda p: gather(p, 2))
    run(a, b, lambda p: magnetic(p, 3))
    run(a + 1, b, lambda p: electric(p, 3))
    run(a + 1, b, lambda p: gather(p, 3))
    magnetic(a + 1, 4)

    for copy in first_told:
        copy.arrived()
    unfold(1)
    each((0, top), lambda p: magnetic(p, 2))
    each((0, 1, top), lambda p: electric(p, 2))
    each((1, b), lambda p: magnetic(p, 3))
    each((a, b), lambda p: electric(p, 3))
    each((a, b), lambda p: gather(p, 3))
    each((a, b - 1), lambda p: magnetic(p, 4))
    each((a + 1, b - 1), lambda p: electric(p, 4))
    each((a + 1, b - 1), lambda p: gather(p, 4))

    stores = []

    def store(planes_at):
        for k, (src, dst) in enumerate(((out_ref, out), (grad_ref, grad))):
            there = (slice(None), planes_at) if k == 0 else (planes_at,)
            stores.append(
                pltpu.make_async_copy(src.at[there], dst.at[there], local.at[4 + len(stores)])
            )
            stores[-1].start()

    store(pl.ds(1, depth - 2))
    for side, copies, outermost, block in ((1, told_down, top, b), (0, told_up, 0, a)):
        for copy in copies:
            copy.arrived()
        unfold(2, (side,))
        magnetic(outermost, 3)
        electric(top if side else 1, 3)
        magnetic(b if side else 1, 4)
        electric(block, 4)
        gather(block, 4)
        store(pl.ds(block - LOW, 1))
    for copy in stores:
        copy.wait()
    for copy in planes + outer + tiles + columns + ghosts + corners + borders + first_told + told_up + told_down:
        copy.sent()


def hand_on(fields, grad, fields_out, grad_out, staged, staged_grad, sem):
    depth = grad.shape[0]
    parts = [(grad, staged_grad, grad_out)]
    for c in range(6):
        for p in range(0, depth, 2):
            at = (c, pl.ds(p, 2))
            parts.append((fields.at[at], staged.at[at], fields_out.at[at]))
    inward = [pltpu.make_async_copy(a, b, sem.at[k]) for k, (a, b, _) in enumerate(parts)]
    outward = [pltpu.make_async_copy(b, c, sem.at[len(parts) + k]) for k, (_, b, c) in enumerate(parts)]
    for copy in inward:
        copy.start()
    for one, two in zip(inward, outward):
        one.wait()
        two.start()
    for copy in outward:
        copy.wait()


def on_device(
    fields_in, material, material_eps, source_plane, source_wave, source_profile, forward_fields
):
    depth, rows, lanes = material.shape
    wide = rows + 2 * HALO
    levels = depth + 2 * LOW
    f32 = jnp.float32
    scalars = pl.BlockSpec(memory_space=pltpu.SMEM)
    remote = pl.BlockSpec(memory_space=pltpu.HBM)
    fields_out, eps_grad = pl.pallas_call(
        kernel,
        out_shape=(
            jax.ShapeDtypeStruct(fields_in.shape, f32),
            jax.ShapeDtypeStruct(material.shape, f32),
        ),
        in_specs=[scalars] * 3 + [remote] * 4,
        out_specs=(remote, remote),
        scratch_shapes=[
            pltpu.VMEM(fields_in.shape, f32),
            pltpu.VMEM(material.shape, f32),
            pltpu.VMEM((6, levels, wide, lanes), f32),
            pltpu.VMEM((6, levels, wide, lanes), f32),
            pltpu.VMEM((levels, wide, lanes), f32),
            pltpu.VMEM((levels, wide, lanes), f32),
            pltpu.VMEM((levels, wide, lanes), jnp.int32),
            pltpu.VMEM((wide, lanes), f32),
            pltpu.VMEM((wide, lanes), f32),
            pltpu.VMEM(forward_fields.shape, forward_fields.dtype),
            pltpu.VMEM((2, rows, lanes), f32),
            pltpu.VMEM((2, 2, rows, lanes), f32),
            pltpu.VMEM((2, wide, lanes), f32),
            pltpu.VMEM((2, wide, lanes), f32),
            pltpu.VMEM((2, 6, depth // 2, 8, lanes), f32),
            pltpu.VMEM((2, depth // 2, 8, lanes), jnp.int32),
            pltpu.VMEM((2, 6, depth, 8, lanes), f32),
            pltpu.VMEM((2, 6, depth // 2, 8, lanes), f32),
            pltpu.VMEM((2, depth // 2, 8, lanes), jnp.int32),
            pltpu.VMEM((2, 8, lanes), f32),
            pltpu.VMEM((2, 2, 2, 8, lanes), f32),
            pltpu.VMEM((6, depth, 8, lanes), f32),
            pltpu.VMEM((depth, 8, lanes), jnp.int32),
            pltpu.VMEM((2, 2, 2 * wide + 16, lanes), f32),
            pltpu.VMEM((2, 2, 2 * wide + 16, lanes), f32),
            pltpu.VMEM((2, 2, 2, wide, lanes), f32),
            pltpu.SemaphoreType.DMA((12,)),
            pltpu.SemaphoreType.DMA((COPIES,)),
            pltpu.SemaphoreType.DMA((COPIES,)),
        ],
        compiler_params=pltpu.CompilerParams(
            collective_id=0, has_side_effects=True, vmem_limit_bytes=60 << 20
        ),
    )(
        material_eps,
        source_plane,
        source_wave,
        fields_in,
        material,
        source_profile,
        forward_fields,
    )
    return pl.pallas_call(
        hand_on,
        out_shape=(
            jax.ShapeDtypeStruct(fields_in.shape, f32),
            jax.ShapeDtypeStruct(material.shape, f32),
        ),
        in_specs=[remote] * 2,
        out_specs=(remote, remote),
        scratch_shapes=[
            pltpu.VMEM(fields_in.shape, f32),
            pltpu.VMEM(material.shape, f32),
            pltpu.SemaphoreType.DMA((26,)),
        ],
        compiler_params=pltpu.CompilerParams(vmem_limit_bytes=60 << 20),
    )(fields_out, eps_grad)


def solution(mesh):
    placed = (
        P(None, "gz", "gx", "gy"),
        P("gz", "gx", "gy"),
        P(),
        P(),
        P(),
        P("gx", "gy"),
        P(None, None, "gz", "gx", "gy"),
    )
    return jax.shard_map(
        on_device,
        mesh=mesh,
        in_specs=placed,
        out_specs=(P(None, "gz", "gx", "gy"), P("gz", "gx", "gy")),
        check_vma=False,
    )
```

```python
import functools

import jax
import jax.numpy as jnp
from jax import lax
from jax.experimental import pallas as pl
from jax.experimental.pallas import tpu as pltpu
from jax.sharding import PartitionSpec as P

COURANT = 0.5
MESH = pl.DeviceIdType.MESH
STEPS = 4
LOW = 2
HALO = 4
SLOT = 2 * HALO
COPIES = 31
CHIPS_Z = 16


def around(axis, by):
    size = lax.axis_size(axis)
    return lax.rem(lax.axis_index(axis) + by + size, size)


class Copy:
    def __init__(self, k, src, dst, send, recv, **steps):
        self.end = "gz" in steps
        by = steps.get("gz", 1)
        last = lax.axis_size("gz") - 1
        self.sends = lax.axis_index("gz") != (last if by > 0 else 0)
        self.takes = lax.axis_index("gz") != (0 if by > 0 else last)
        self.copy = pltpu.make_async_remote_copy(
            src_ref=src,
            dst_ref=dst,
            send_sem=send.at[k],
            recv_sem=recv.at[k],
            device_id={axis: around(axis, n) for axis, n in steps.items()},
            device_id_type=MESH,
        )

    def _on(self, flag, act):
        if self.end:
            pl.when(flag)(act)
        else:
            act()

    def start(self):
        self._on(self.sends, self.copy.start)

    def sent(self):
        self._on(self.sends, self.copy.wait_send)

    def arrived(self):
        self._on(self.takes, self.copy.wait_recv)


def each(planes, act):
    for p in planes:
        act(p)


def run(lo, hi, act):
    if hi - lo == 1:
        act(lo)
    else:
        lax.fori_loop(lo, hi, lambda p, _: (act(p), 0)[1], 0)


def kernel(
    eps_ref,
    plane_ref,
    wave_ref,
    fields,
    material,
    profile,
    forward,
    out,
    grad,
    out_ref,
    grad_ref,
    fa,
    fb,
    ca,
    cb,
    mat,
    prof_a,
    prof_b,
    stored,
    packed,
    y_in,
    border,
    z_border,
    x_pack,
    x_mat_pack,
    near,
    x_in,
    x_mat_in,
    x_prof_in,
    x_border_in,
    x_out,
    x_mat_out,
    said,
    heard,
    heard_b,
    local,
    send,
    recv,
):
    _, depth, rows, lanes = fields.shape
    wide = rows + 2 * HALO
    own = pl.ds(0, rows)
    extra = pl.ds(rows, 2 * HALO)
    first, final = pl.ds(0, 8), pl.ds(rows - 8, 8)
    top = LOW + depth
    gz, last = lax.axis_index("gz"), lax.axis_size("gz") - 1
    make = functools.partial(Copy, send=send, recv=recv)

    barrier = pltpu.get_barrier_semaphore()

    def greet(**steps):
        there = {axis: around(axis, n) for axis, n in steps.items()}
        pl.semaphore_signal(barrier, inc=1, device_id=there, device_id_type=MESH)

    pl.when(gz != last)(lambda: greet(gz=1))
    pl.when(gz != 0)(lambda: greet(gz=-1))
    for by in (1, -1):
        greet(gx=by)
        greet(gy=by)
        for n in (1, -1):
            greet(gx=by, gy=n)
    loads = [
        pltpu.make_async_copy(src, dst, local.at[k])
        for k, (src, dst) in enumerate(
            (
                (fields, fa.at[:, pl.ds(LOW, depth), own]),
                (material, mat.at[pl.ds(LOW, depth), own]),
                (profile, prof_a.at[own]),
                (forward, stored),
            )
        )
    ]
    edges = [
        pltpu.make_async_copy(fields.at[:, :, edge], near.at[k], local.at[10 + k])
        for k, edge in enumerate((first, final))
    ]
    for load in edges + [loads[1], loads[0], loads[2]]:
        load.start()
    edge = (gz == 0) | (gz == last)
    pl.semaphore_wait(barrier, jnp.where(edge, 9, 10))

    falling = [
        make(9, fields.at[:, 0], fa.at[:, top, own], gz=-1),
        make(12, material.at[0], mat.at[top, own], gz=-1),
    ]
    rising = [
        make(0, fields.at[:, depth - 1], fa.at[:, 1, own], gz=1),
        make(2, material.at[pl.ds(depth - 2, 2)], mat.at[pl.ds(0, 2), own], gz=1),
    ]
    outer = [
        make(1, fields.at[pl.ds(0, 5), depth - 2], fa.at[pl.ds(0, 5), 0, own], gz=1),
        make(11, fields.at[pl.ds(0, 2), 1], fa.at[pl.ds(0, 2), top + 1, own], gz=-1),
    ]
    planes = falling + rising
    turn = gz % CHIPS_Z == 0
    for copy in rising:
        copy.start()

    @pl.when(~turn)
    def _():
        for copy in falling:
            copy.start()

    lane = lax.broadcasted_iota(jnp.int32, (wide, lanes), 1)
    tile_row = lax.broadcasted_iota(jnp.int32, (8, lanes), 0)
    from_next = tile_row < HALO
    at_first, at_last = lane == 0, lane == lanes - 1

    for load in edges + [loads[1]]:
        load.wait()

    def turned(tile):
        return pltpu.roll(tile, HALO, 0)

    tiles = []
    for k, (by, edge) in enumerate(((-1, first), (1, final))):
        for h in range(depth // 2):
            p = LOW + 2 * h
            pairs = [(near[k, c, 2 * h], near[k, c, 2 * h + 1], x_pack.at[k, c, h]) for c in range(6)]
            for one, two, dest in pairs + [(mat[p, edge], mat[p + 1, edge], x_mat_pack.at[k, h])]:
                one, two = (one, turned(two)) if k == 0 else (turned(one), two)
                dest[...] = jnp.where(from_next, one, two)
        tiles += [
            make(19 + 3 * k, x_pack.at[k], x_in.at[k], gx=by),
            make(20 + 3 * k, x_mat_pack.at[k], x_mat_in.at[k], gx=by),
            make(21 + 3 * k, profile.at[edge], x_prof_in.at[k], gx=by),
        ]
    for copy in tiles:
        copy.start()
    loads[0].wait()
    loads[2].wait()

    def narrow(c, p):
        return mat[LOW + p, own].astype(jnp.float32) if c == 6 else fa[c, LOW + p, own]

    def place(c, p):
        return p // 2, 7 * (p % 2) + c

    profile_place = (0, 14)
    slot_of = lane[:rows] // SLOT
    for half in range(2):
        filled = jnp.zeros((rows, lanes), jnp.float32)
        pieces = [(place(c, p)[1], narrow(c, p)) for p in (2 * half, 2 * half + 1) for c in range(7)]
        if half == profile_place[0]:
            pieces.append((profile_place[1], prof_a[own]))
        for s, value in pieces:
            filled = jnp.where(slot_of == s, pltpu.roll(value, SLOT * s + HALO, 1), filled)
        packed[half] = filled
    columns = [make(29 + k, packed, y_in.at[k], gy=by) for k, by in enumerate((-1, 1))]
    corners = [
        make(25 + 2 * k + n, packed.at[:, edge], x_border_in.at[k, n], gx=by, gy=way)
        for k, (by, edge) in enumerate(((-1, first), (1, final)))
        for n, way in enumerate((-1, 1))
    ]
    for copy in corners + columns:
        copy.start()
    loads[3].start()

    @pl.when(gz == 0)
    def _():
        fa[:, pl.ds(0, LOW)] = jnp.zeros((6, LOW, wide, lanes), jnp.float32)
        mat[pl.ds(0, LOW)] = jnp.zeros((LOW, wide, lanes), jnp.int32)
        z_border[0] = jnp.zeros(z_border.shape[1:], jnp.float32)
        for m in range(2):
            heard[m, 0] = jnp.zeros(heard.shape[2:], jnp.float32)

    @pl.when(gz == last)
    def _():
        fa[:, pl.ds(top, 2)] = jnp.zeros((6, 2, wide, lanes), jnp.float32)
        mat[top] = jnp.zeros((wide, lanes), jnp.int32)
        z_border[1] = jnp.zeros(z_border.shape[1:], jnp.float32)
        for m in range(2):
            heard[m, 1] = jnp.zeros(heard.shape[2:], jnp.float32)

    for copy in tiles:
        copy.arrived()

    @pl.when(turn)
    def _():
        for copy in falling:
            copy.start()

    def meet(after, before, p):
        after, before = (turned(after), before) if p % 2 else (after, turned(before))
        return jnp.where(from_next, after, before)

    for c in range(6):
        for p in range(depth):
            tile = meet(x_in[0, c, p // 2], x_in[1, c, p // 2], p)
            x_out[c, p] = tile
            fa[c, LOW + p, extra] = tile
    for p in range(depth):
        tile = meet(x_mat_in[0, p // 2], x_mat_in[1, p // 2], p)
        x_mat_out[p] = tile
        mat[LOW + p, extra] = tile
    prof_a[extra] = jnp.where(from_next, x_prof_in[0], x_prof_in[1])
    ghosts = [
        make(13, x_out.at[:, 0], fa.at[:, top, extra], gz=-1),
        make(15, x_mat_out.at[0], mat.at[top, extra], gz=-1),
        make(3, x_out.at[:, depth - 1], fa.at[:, 1, extra], gz=1),
        make(5, x_mat_out.at[pl.ds(depth - 2, 2)], mat.at[pl.ds(0, 2), extra], gz=1),
    ]
    outer += [
        make(4, x_out.at[pl.ds(0, 5), depth - 2], fa.at[pl.ds(0, 5), 0, extra], gz=1),
        make(14, x_out.at[pl.ds(0, 2), 1], fa.at[pl.ds(0, 2), top + 1, extra], gz=-1),
    ]
    for copy in ghosts:
        copy.start()

    for copy in columns:
        copy.arrived()
    from_below = lane % SLOT < HALO
    for half in range(2):
        border[half, own] = jnp.where(from_below[:rows], y_in[1, half], y_in[0, half])
    table = [COURANT / jnp.full((1, lanes), eps_ref[m], jnp.float32) for m in range(eps_ref.shape[0])]

    def coef_a(p, keep=None):
        kinds = mat[p]
        value = jnp.broadcast_to(table[0], (wide, lanes))
        for m in range(1, len(table)):
            value = jnp.where(kinds == m, table[m], value)
        ca[p] = value if keep is None else value * keep

    def coef_b(p, kinds, keep=None):
        value = jnp.broadcast_to(table[0], kinds.shape)
        for m in range(1, len(table)):
            value = jnp.where(kinds > m - 0.5, table[m], value)
        cb[p] = value if keep is None else value * keep

    def unpack(value, s):
        return pltpu.roll(value, lanes - (SLOT * s + HALO), 1)

    run(LOW, top, coef_a)
    for copy in corners:
        copy.arrived()
    for half in range(2):
        tile = jnp.where(from_next, x_border_in[0, :, half], x_border_in[1, :, half])
        border[half, extra] = jnp.where(from_below[:8], tile[1], tile[0])
    borders = [
        make(6, border.at[1], z_border.at[0], gz=1),
        make(16, border.at[0], z_border.at[1], gz=-1),
    ]
    for copy in borders + outer:
        copy.start()

    for p in range(depth):
        for c in range(6):
            fb[c, LOW + p] = unpack(border[place(c, p)[0]], place(c, p)[1])
        coef_b(LOW + p, unpack(border[place(6, p)[0]], place(6, p)[1]))
    prof_b[...] = unpack(border[profile_place[0]], profile_place[1])

    low_rate = COURANT * (gz != 0).astype(jnp.float32)

    def pair(c, p, t=0):
        if t > 0 and c < 2 and isinstance(p, int) and p in (0, top + 1):
            side = 0 if p == 0 else 1
            return heard[t - 1, side, pl.ds(c * wide, wide)], heard_b[t - 1, side, c]
        return fa[c, p], fb[c, p]

    def minus(u, v):
        return u[0] - v[0], u[1] - v[1]

    def next_x(u):
        return tuple(pltpu.roll(v, wide - 1, 0) - v for v in u)

    def last_x(u):
        return tuple(v - pltpu.roll(v, 1, 0) for v in u)

    def next_y(u):
        a, b = (pltpu.roll(v, lanes - 1, 1) for v in u)
        return jnp.where(at_last, b, a) - u[0], jnp.where(at_last, a, b) - u[1]

    def last_y(u):
        a, b = (pltpu.roll(v, 1, 1) for v in u)
        return u[0] - jnp.where(at_first, b, a), u[1] - jnp.where(at_first, a, b)

    def put(c, p, value, t):
        fa[c, p] = value[0]
        if t < STEPS or c > 2:
            fb[c, p] = value[1]
        if t == STEPS and not (isinstance(p, int) and not LOW <= p < top):
            out_ref[c, p - LOW] = value[0][:rows]

    def magnetic(p, t):
        low = isinstance(p, int) and p < LOW
        rate = low_rate if low else COURANT
        outer = isinstance(p, int) and (p == 0 or p < LOW and t == STEPS)

        def push(c, curl):
            old = fa[c, p], fb[c, p]
            put(c, p, tuple(o - rate * k for o, k in zip(old, curl)), t)

        ex, ey, ez = pair(0, p, t - 1), pair(1, p, t - 1), pair(2, p)
        push(3, minus(next_y(ez), minus(pair(1, p + 1, t - 1), ey)))
        push(4, minus(minus(pair(0, p + 1, t - 1), ex), next_x(ez)))
        if not outer:
            push(5, minus(next_x(ey), next_y(ex)))

    def electric(p, t, along=(0, 1, 2)):
        coef = ca[p], cb[p]

        def push(c, curl):
            old = fa[c, p], fb[c, p]
            put(c, p, tuple(o + k * d for o, k, d in zip(old, coef, curl)), t)

        hx, hy = pair(3, p), pair(4, p)
        if 2 in along and not (isinstance(p, int) and p == top and t == STEPS - 1):
            push(2, minus(last_x(hy), last_y(hx)))
        if 0 not in along or isinstance(p, int) and p == 0:
            return
        hz = pair(5, p)
        here = (gz * depth + p - LOW == plane_ref[0]).astype(jnp.float32)
        pushed = wave_ref[t - 1] * here
        curl = minus(last_y(hz), minus(hy, pair(4, p - 1)))
        push(0, (curl[0] + pushed * prof_a[...], curl[1] + pushed * prof_b[...]))
        push(1, minus(minus(hx, pair(3, p - 1)), last_x(hz)))

    def gather(p, t):
        total = jnp.zeros((rows, lanes), jnp.float32) if t == 1 else grad_ref[p - LOW]
        for c in range(3):
            total = total + stored[t - 1, c, p - LOW].astype(jnp.float32) * fa[c, p, own]
        if t == STEPS:
            total = jnp.where(mat[p, own] >= 2, -total, 0.0)
        grad_ref[p - LOW] = total

    folds = lanes // (2 * SLOT)
    fold = ((lane[:8] + HALO) % lanes) // (2 * SLOT)

    def unfold(t, sides=(0, 1)):
        for side in sides:
            for i in range(folds + 1):
                part = heard[t - 1, side, pl.ds(2 * wide + 8 * (i // folds), 8)]
                for c in range(2):
                    by = (2 * SLOT * (i % folds) + SLOT * c) % lanes
                    heard_b[t - 1, side, c, pl.ds(8 * i, 8)] = (
                        pltpu.roll(part, lanes - by, 1) if by else part
                    )

    def tell(t, sides=(0, 1)):
        copies = []
        for k in sides:
            p, by = ((top - 2, 1), (LOW + 1, -1))[k]
            words = said.at[t - 1, k]
            words[pl.ds(0, wide)], words[pl.ds(wide, wide)] = fa[0, p], fa[1, p]
            ghost = jnp.where(
                (lane >= HALO) & (lane < HALO + SLOT), pltpu.roll(fb[1, p], SLOT, 1), fb[0, p]
            )
            filled = ghost[:8]
            for i in range(1, folds):
                turn_by = 2 * SLOT * i
                part = pltpu.roll(ghost[8 * i : 8 * i + 8], turn_by, 1)
                filled = jnp.where(fold == i, part, filled)
            words[pl.ds(2 * wide, 8)] = filled
            words[pl.ds(2 * wide + 8, 8)] = ghost[8 * folds :]
            copies.append(make(7 + 10 * k - 1 + t, words, heard.at[t - 1, k], gz=by))
        for copy in copies:
            copy.start()
        return copies

    a, b = LOW, top - 1
    run(a, b, lambda p: magnetic(p, 1))
    run(a + 1, b, lambda p: electric(p, 1))
    first_told = tell(1)
    loads[3].wait()
    run(a + 1, b, lambda p: gather(p, 1))

    magnetic(a + 1, 2)

    for copy in falling + ghosts[:2] + borders[1:]:
        copy.arrived()
    for c in range(6):
        fb[c, top] = unpack(z_border[1], place(c, 0)[1])
    magnetic(b, 1)
    electric(b, 1)
    magnetic(b - 1, 2)
    electric(b - 1, 2, (0, 1))
    told_up = tell(2, (0,))

    for copy in rising + ghosts[2:] + borders[:1]:
        copy.arrived()
    coef_a(1)
    for c in range(6):
        fb[c, 1] = unpack(z_border[0], place(c, depth - 1)[1])
    coef_b(1, unpack(z_border[0], place(6, depth - 1)[1]))
    magnetic(1, 1)
    electric(a, 1)
    magnetic(a, 2)
    electric(a + 1, 2, (0, 1))
    told_down = tell(2, (1,))
    each((a + 1, b - 1), lambda p: electric(p, 2, (2,)))
    each((a, b), lambda p: gather(p, 1))
    run(a + 1, b, lambda p: gather(p, 2))

    for copy in outer:
        copy.arrived()
    keep = (gz != last).astype(jnp.float32)
    coef_a(0)
    coef_a(top, keep)
    for c in range(5):
        fb[c, 0] = unpack(z_border[0], place(c, depth - 2)[1])
    coef_b(0, unpack(z_border[0], place(6, depth - 2)[1]))
    coef_b(top, unpack(z_border[1], place(6, 0)[1]), keep)
    for c in range(2):
        fb[c, top + 1] = unpack(z_border[1], place(c, 1)[1])
    each((0, top), lambda p: magnetic(p, 1))
    each((0, 1, top), lambda p: electric(p, 1))
    each((1, b), lambda p: magnetic(p, 2))
    each((a, b), lambda p: electric(p, 2))
    each((a, b), lambda p: gather(p, 2))
    run(a, b, lambda p: magnetic(p, 3))
    run(a + 1, b, lambda p: electric(p, 3))
    run(a + 1, b, lambda p: gather(p, 3))
    magnetic(a + 1, 4)

    for copy in first_told:
        copy.arrived()
    unfold(1)
    each((0, top), lambda p: magnetic(p, 2))
    each((0, 1, top), lambda p: electric(p, 2))
    each((1, b), lambda p: magnetic(p, 3))
    each((a, b), lambda p: electric(p, 3))
    each((a, b), lambda p: gather(p, 3))
    each((a, b - 1), lambda p: magnetic(p, 4))
    each((a + 1, b - 1), lambda p: electric(p, 4))
    each((a + 1, b - 1), lambda p: gather(p, 4))

    stores = []

    def store(planes_at):
        for k, (src, dst) in enumerate(((out_ref, out), (grad_ref, grad))):
            there = (slice(None), planes_at) if k == 0 else (planes_at,)
            stores.append(
                pltpu.make_async_copy(src.at[there], dst.at[there], local.at[4 + len(stores)])
            )
            stores[-1].start()

    store(pl.ds(1, depth - 2))
    for side, copies, outermost, block in ((1, told_down, top, b), (0, told_up, 0, a)):
        for copy in copies:
            copy.arrived()
        unfold(2, (side,))
        magnetic(outermost, 3)
        electric(top if side else 1, 3)
        magnetic(b if side else 1, 4)
        electric(block, 4)
        gather(block, 4)
        store(pl.ds(block - LOW, 1))
    for copy in stores:
        copy.wait()
    for copy in planes + outer + tiles + columns + ghosts + corners + borders + first_told + told_up + told_down:
        copy.sent()


def hand_on(fields, grad, fields_out, grad_out, staged, staged_grad, sem):
    depth = grad.shape[0]
    parts = [(grad, staged_grad, grad_out)]
    for c in range(6):
        for p in range(0, depth, 2):
            at = (c, pl.ds(p, 2))
            parts.append((fields.at[at], staged.at[at], fields_out.at[at]))
    inward = [pltpu.make_async_copy(a, b, sem.at[k]) for k, (a, b, _) in enumerate(parts)]
    outward = [pltpu.make_async_copy(b, c, sem.at[len(parts) + k]) for k, (_, b, c) in enumerate(parts)]
    for copy in inward:
        copy.start()
    for one, two in zip(inward, outward):
        one.wait()
        two.start()
    for copy in outward:
        copy.wait()


def on_device(
    fields_in, material, material_eps, source_plane, source_wave, source_profile, forward_fields
):
    depth, rows, lanes = material.shape
    wide = rows + 2 * HALO
    levels = depth + 2 * LOW
    f32 = jnp.float32
    scalars = pl.BlockSpec(memory_space=pltpu.SMEM)
    remote = pl.BlockSpec(memory_space=pltpu.HBM)
    fields_out, eps_grad = pl.pallas_call(
        kernel,
        out_shape=(
            jax.ShapeDtypeStruct(fields_in.shape, f32),
            jax.ShapeDtypeStruct(material.shape, f32),
        ),
        in_specs=[scalars] * 3 + [remote] * 4,
        out_specs=(remote, remote),
        scratch_shapes=[
            pltpu.VMEM(fields_in.shape, f32),
            pltpu.VMEM(material.shape, f32),
            pltpu.VMEM((6, levels, wide, lanes), f32),
            pltpu.VMEM((6, levels, wide, lanes), f32),
            pltpu.VMEM((levels, wide, lanes), f32),
            pltpu.VMEM((levels, wide, lanes), f32),
            pltpu.VMEM((levels, wide, lanes), jnp.int32),
            pltpu.VMEM((wide, lanes), f32),
            pltpu.VMEM((wide, lanes), f32),
            pltpu.VMEM(forward_fields.shape, forward_fields.dtype),
            pltpu.VMEM((2, rows, lanes), f32),
            pltpu.VMEM((2, 2, rows, lanes), f32),
            pltpu.VMEM((2, wide, lanes), f32),
            pltpu.VMEM((2, wide, lanes), f32),
            pltpu.VMEM((2, 6, depth // 2, 8, lanes), f32),
            pltpu.VMEM((2, depth // 2, 8, lanes), jnp.int32),
            pltpu.VMEM((2, 6, depth, 8, lanes), f32),
            pltpu.VMEM((2, 6, depth // 2, 8, lanes), f32),
            pltpu.VMEM((2, depth // 2, 8, lanes), jnp.int32),
            pltpu.VMEM((2, 8, lanes), f32),
            pltpu.VMEM((2, 2, 2, 8, lanes), f32),
            pltpu.VMEM((6, depth, 8, lanes), f32),
            pltpu.VMEM((depth, 8, lanes), jnp.int32),
            pltpu.VMEM((2, 2, 2 * wide + 16, lanes), f32),
            pltpu.VMEM((2, 2, 2 * wide + 16, lanes), f32),
            pltpu.VMEM((2, 2, 2, wide, lanes), f32),
            pltpu.SemaphoreType.DMA((12,)),
            pltpu.SemaphoreType.DMA((COPIES,)),
            pltpu.SemaphoreType.DMA((COPIES,)),
        ],
        compiler_params=pltpu.CompilerParams(
            collective_id=0, has_side_effects=True, vmem_limit_bytes=60 << 20
        ),
    )(
        material_eps,
        source_plane,
        source_wave,
        fields_in,
        material,
        source_profile,
        forward_fields,
    )
    return pl.pallas_call(
        hand_on,
        out_shape=(
            jax.ShapeDtypeStruct(fields_in.shape, f32),
            jax.ShapeDtypeStruct(material.shape, f32),
        ),
        in_specs=[remote] * 2,
        out_specs=(remote, remote),
        scratch_shapes=[
            pltpu.VMEM(fields_in.shape, f32),
            pltpu.VMEM(material.shape, f32),
            pltpu.SemaphoreType.DMA((26,)),
        ],
        compiler_params=pltpu.CompilerParams(vmem_limit_bytes=60 << 20),
    )(fields_out, eps_grad)


def solution(mesh):
    placed = (
        P(None, "gz", "gx", "gy"),
        P("gz", "gx", "gy"),
        P(),
        P(),
        P(),
        P("gx", "gy"),
        P(None, None, "gz", "gx", "gy"),
    )
    return jax.shard_map(
        on_device,
        mesh=mesh,
        in_specs=placed,
        out_specs=(P(None, "gz", "gx", "gy"), P("gz", "gx", "gy")),
        check_vma=False,
    )
```
